128 devices in a mesh: pix: 8 (over y, core), exp: 16 (over x, z).
Axes of the slice: x: 4, y: 4, z: 4, core: 2. Of those that a mesh axis runs over, the one named last changes fastest.
Arguments:
- design: bfloat16 [200, 786432], P(None, ('pix', 'exp')), may hold values from -1 to 1
- det_weight: float32 [786432], P(('pix', 'exp')), may hold values from 0.2 to 2
- outlier_mask: int32 [2, 786432], P(None, ('pix', 'exp')), may hold values from 0 to 1
- star_owner: int32 [786432, 1], P(('pix', 'exp')), may hold values from 0 to 127; in each aligned block of 6144 rows (0 to 6143, 6144 to 12287, ...) at most 96 rows name the same one
- star_slot: int32 [786432], P(('pix', 'exp')), may hold values from 0 to 767
- coef_init: float32 [128, 2, 200], P('exp'), may hold values from -6 to 6
- star_ref: float32 [2, 98304], P(None, ('pix', 'exp')), may hold values from -24 to 24
- star_prior: float32 [98304], P(('pix', 'exp')), may hold values from 0.2 to 2
Outputs:
- coefficients: float32 [128, 2, 200], P('exp')
- star_means: float32 [2, 98304], P(None, ('pix', 'exp'))
The draws below stay inside these ranges and needn't reach their ends.
Inputs may be any that keep to these rules, and one draw needn't show every extreme that they name: `star_owner`: among the 6144 detections of one device, at most 96 name the same owner, and in every draw some device's detections name some owner exactly 96 times.
All inputs are finite; a program needn't handle non-finite values.
Results may differ from the reference program's by a relative error of at most 0.00045.
The reference program's roundings to bfloat16 on the way count: a program that leaves them out, or rounds other values in their place, can miss the bound.
Values sent between devices are 32-bit elements; how exact they have to be, the bound alone decides.
No kernel may reach another device: no remote copies, remote signals or barrier semaphores. Data moves between devices by JAX's collectives and lax.ppermute only.
A program may use at most 64 MiB of HBM per device.

```python
import math
import jax
import jax.numpy as jnp
import numpy as np
from jax import lax

NTERM = 200
EXP_DEV = 8
ROWS_DEV = 6144
ITERS = 2
EXP_ROWS = 768
EXP_DET = 6144
DETECTIONS = 786432
EXPOSURES = 128
STAR_DEV = 768
STARS = 98304
CAP = 96
N_PIX = 8
N_EXP = 16
DEVICES = 128


def term_exponents(term_count):
    first_powers = []
    second_powers = []
    degree = 0
    while len(first_powers) < term_count:
        for exponent in range(degree, -1, -1):
            if len(first_powers) < term_count:
                first_powers.append(exponent)
                second_powers.append(degree - exponent)
        degree = degree + 1
    return (first_powers, second_powers, degree)


def power_table(position, top_degree):
    powers = [jnp.ones_like(position)]
    for exponent in range(1, top_degree):
        powers.append(powers[-1] * position)
    return powers


def draw_design(key, part):
    first_powers, second_powers, top_degree = term_exponents(NTERM)
    place_key = jax.random.fold_in(key, 11)
    across = jax.random.uniform(jax.random.fold_in(place_key, 1), (DETECTIONS,), jnp.float32, -1.0, 1.0)
    along = jax.random.uniform(jax.random.fold_in(place_key, 2), (DETECTIONS,), jnp.float32, -1.0, 1.0)
    table_across = power_table(across, top_degree)
    table_along = power_table(along, top_degree)
    rows_out = []
    for index in range(NTERM):
        first_power = first_powers[index]
        second_power = second_powers[index]
        factor = float(np.sqrt((2.0 * first_power + 1.0) * (2.0 * second_power + 1.0) / EXP_DET))
        term_row = table_across[first_power] * table_along[second_power] * factor
        rows_out.append(term_row.astype(jnp.bfloat16))
    return jnp.stack(rows_out, axis=0)


def draw_outlier_mask(key, part):
    mask_key = jax.random.fold_in(key, 23)
    classes = jax.random.randint(jax.random.fold_in(mask_key, 1), (EXPOSURES,), 0, 4)
    rounds = jnp.arange(ITERS, dtype=jnp.int32)[:, None]
    first_round = rounds == 0
    keep_counts = jnp.where(classes[None, :] == 0, jnp.where(first_round, 1, 7), jnp.where(classes[None, :] == 1, jnp.where(first_round, 7, 1), 7))
    detection = jnp.arange(DETECTIONS, dtype=jnp.int32)
    exposure = detection // ROWS_DEV % (EXPOSURES // EXP_DEV) * EXP_DEV + detection % ROWS_DEV // EXP_ROWS
    dice_rolls = jax.random.randint(jax.random.fold_in(mask_key, 2), (ITERS, DETECTIONS), 0, 8)
    return (dice_rolls < keep_counts[:, exposure]).astype(jnp.int32)


def touch_ends(array, stream_key, smallest, top_value):
    longest = array.shape.index(max(array.shape))
    spots = []
    for shift in (0, 1):
        where = [jax.random.randint(jax.random.fold_in(stream_key, axis), (), 0, length) for axis, length in enumerate(array.shape)]
        where[longest] = (where[longest] + shift) % array.shape[longest]
        spots.append(tuple(where))
    return array.at[spots[0]].set(smallest).at[spots[1]].set(top_value)


def steps_of(stream_key, dims, pieces, low, top_value):
    level, own = 1.0, jax.random.fold_in(stream_key, 6)
    for dim, parts in pieces:
        draws = jnp.exp(jax.random.uniform(jax.random.fold_in(own, dim), (parts,), jnp.float32, low / len(pieces), top_value / len(pieces)))
        level = level * jnp.repeat(draws, dims[dim] // parts).reshape([-1 if axis == dim else 1 for axis in range(len(dims))])
    return level


def assign_block(stream_key, own, number, rows, amount, top, reach, slope):
    order = jax.random.permutation(stream_key, amount)
    crowded, common = load_shares(amount, rows * top, reach, slope, True), load_shares(amount, rows * top, reach, slope, False)
    places = jnp.arange(amount)

    def named(sizes, rotation):
        used = int((sizes > 0).sum())
        fixed = max(1, used // 4)
        passed = fixed + (places - fixed + rotation * (used - fixed)) % max(1, amount - fixed)
        return jnp.zeros((amount,), jnp.int32).at[order[jnp.where(places < fixed, places, passed)]].set(jnp.asarray(sizes, jnp.int32))

    sizes = jnp.where(number % 4 == 0, named(crowded, number // 4), named(common, number - number // 4 - 1))
    mixed = jax.random.permutation(jax.random.fold_in(own, 3), amount)
    source_of, taker = mixed[0:amount // 2 * 2:2], mixed[1:amount // 2 * 2:2]
    slack = jnp.minimum(sizes[source_of] - 1, reach - sizes[taker]) // 2
    slack = jnp.where((source_of == order[0]) | (taker == order[0]) | (sizes[taker] == 0), 0, jnp.maximum(slack, 0))
    passed = jax.random.randint(jax.random.fold_in(own, 4), (amount // 2,), 0, 1 << 20) % (slack + 1)
    sizes = sizes.at[source_of].add(-passed).at[taker].add(passed)
    labels = jnp.searchsorted(jnp.cumsum(sizes), jnp.arange(rows * top), side="right").astype(jnp.int32)
    grid = labels.reshape(top, rows).T
    grid = grid[jax.random.permutation(jax.random.fold_in(own, 1), rows)]
    rotation = jax.random.randint(jax.random.fold_in(own, 2), (rows, 1), 0, top)
    return jnp.take_along_axis(grid, (jnp.arange(top)[None, :] + rotation) % top, axis=1)


def load_shares(number_of, total, reach, lean, full):
    weights = [(1 << 20) // math.isqrt(grade ** lean) + 1 for grade in range(1, number_of + 1)]
    largest = reach if full else min(reach, max(-(-total // number_of), total * weights[0] // sum(weights)))
    least = 1 if total - largest >= number_of - 1 else 0
    counts, surplus = [largest] + [least] * (number_of - 1), total - largest - least * (number_of - 1)
    while surplus > 0:
        movable = [i for i in range(1, number_of) if counts[i] < largest] or [i for i in range(1, number_of) if counts[i] < reach]
        mass, left = sum([weights[i] for i in movable]), surplus
        for i in movable:
            extra = min(reach - counts[i], max(1, left * weights[i] // mass), surplus)
            counts[i] = counts[i] + extra
            surplus = surplus - extra
    return np.array(counts)


def gaussian(rng, dims, spread, reach, split=(), held_as=jnp.bfloat16):
    entries = jax.random.normal(rng, dims, jnp.float32) * spread
    if len(split) > 0:
        entries = steps_of(rng, dims, split, -0.22, 0.18) * entries
    return jnp.clip(entries, min=-reach, max=reach).astype(held_as)


def setup_inputs(seed: int = 0) -> dict:
    key_list = jax.random.split(jax.random.key(seed), 9)
    design = draw_design(jax.random.fold_in(key_list[8], 71), 0)
    det_weight = jnp.clip(jnp.exp(math.log(2.0) - 2.3025851 * jax.random.uniform(key_list[1], (DETECTIONS,), jnp.float32) ** steps_of(key_list[1], (DETECTIONS,), ((0, 128),), -0.2, 0.2)), 0.2, 2.0)
    outlier_mask = draw_outlier_mask(jax.random.fold_in(key_list[8], 71), 0)
    star_owner_keys = jax.random.split(jax.random.fold_in(key_list[3], 1), DETECTIONS // ROWS_DEV)
    star_owner_turns = jax.random.permutation(jax.random.fold_in(key_list[3], 3), DETECTIONS // ROWS_DEV)
    star_owner = jax.vmap(lambda own, number: assign_block(jax.random.fold_in(key_list[3], 2), own, number, ROWS_DEV, DEVICES, 1, CAP, 2))(star_owner_keys, star_owner_turns).reshape((DETECTIONS, 1))
    star_slot = touch_ends(jax.random.randint(key_list[4], (DETECTIONS,), 0, STAR_DEV), jax.random.fold_in(key_list[4], 1), 0, STAR_DEV - 1).astype(jnp.int32)
    coef_init = gaussian(key_list[5], (EXPOSURES, 2, NTERM), 1.0, 6.0, ((0, 16),), jnp.float32)
    star_ref = gaussian(key_list[6], (2, STARS), 4.0, 24.0, ((1, 128),), jnp.float32)
    star_prior = jnp.clip(jnp.exp(math.log(2.0) - 2.3025851 * jax.random.uniform(key_list[7], (STARS,), jnp.float32) ** steps_of(key_list[7], (STARS,), ((0, 128),), -0.2, 0.2)), 0.2, 2.0)
    return {"design": design, "det_weight": det_weight, "outlier_mask": outlier_mask, "star_owner": star_owner, "star_slot": star_slot, "coef_init": coef_init, "star_ref": star_ref, "star_prior": star_prior}


RIDGE = 0.5

def solve_blocks(gram_block, right_side):
    identity = jnp.eye(gram_block.shape[-1], dtype=jnp.float32)
    factor = jnp.linalg.cholesky(gram_block + RIDGE * identity)
    columns = jnp.swapaxes(right_side, 1, 2)
    middle = jax.scipy.linalg.solve_triangular(factor, columns, lower=True)
    update = jax.scipy.linalg.solve_triangular(factor, middle, lower=True, trans=1)
    return jnp.swapaxes(update, 1, 2)

def reference(design, det_weight, outlier_mask, star_owner, star_slot, coef_init, star_ref, star_prior):
    blocks = N_PIX * N_EXP
    star_index = star_owner[:, 0] * STAR_DEV + star_slot
    block_ids = jnp.arange(blocks, dtype=jnp.int32)
    coefficients = coef_init
    star_means = jnp.zeros((2, STARS), jnp.float32)
    for step_index in range(ITERS):
        maps_lo = coefficients.astype(jnp.bfloat16)
        masked_weight = det_weight * outlier_mask[step_index].astype(jnp.float32)

        def predict(block_index):
            columns = lax.dynamic_slice_in_dim(design, block_index * ROWS_DEV, ROWS_DEV, 1)
            exp_group = block_index % N_EXP
            local_maps = lax.dynamic_slice_in_dim(maps_lo, exp_group * EXP_DEV, EXP_DEV, 0)
            shaped = columns.astype(jnp.float32).reshape(NTERM, EXP_DEV, EXP_ROWS)
            result = jnp.einsum('jct,tjr->cjr', local_maps.astype(jnp.float32), shaped)
            return result.reshape(2, ROWS_DEV)
        predicted = lax.map(predict, block_ids)
        predicted = jnp.swapaxes(predicted, 0, 1).reshape(2, blocks * ROWS_DEV)
        numerator = jnp.zeros((2, STARS), jnp.float32).at[:, star_index].add(masked_weight[None, :] * predicted)
        denominator = jnp.zeros((STARS,), jnp.float32).at[star_index].add(masked_weight)
        star_means = (star_prior * star_ref + numerator) / (star_prior + denominator)
        residual_lo = (star_means[:, star_index] - predicted).astype(jnp.bfloat16)

        def normal(block_index):
            columns = lax.dynamic_slice_in_dim(design, block_index * ROWS_DEV, ROWS_DEV, 1)
            weight_block = lax.dynamic_slice_in_dim(masked_weight, block_index * ROWS_DEV, ROWS_DEV, 0)
            residual_block = lax.dynamic_slice_in_dim(residual_lo, block_index * ROWS_DEV, ROWS_DEV, 1)
            design_wide = columns.astype(jnp.float32)
            weighted = (design_wide * weight_block[None, :]).astype(jnp.bfloat16)
            weighted_wide = weighted.astype(jnp.float32).reshape(NTERM, EXP_DEV, EXP_ROWS)
            design_wide = design_wide.reshape(NTERM, EXP_DEV, EXP_ROWS)
            gram_block = jnp.einsum('tjr,ujr->jtu', weighted_wide, design_wide)
            residual_wide = residual_block.astype(jnp.float32).reshape(2, EXP_DEV, EXP_ROWS)
            right_side = jnp.einsum('tjr,cjr->jct', weighted_wide, residual_wide)
            return (gram_block, right_side)
        gram_blocks, right_sides = lax.map(normal, block_ids)
        gram_blocks = gram_blocks.reshape(N_PIX, EXPOSURES, NTERM, NTERM).sum(axis=0)
        right_sides = right_sides.reshape(N_PIX, EXPOSURES, 2, NTERM).sum(axis=0)
        coefficients = coefficients + solve_blocks(gram_blocks, right_sides)
    return (coefficients, star_means)
```

```python
import functools

import jax
import jax.numpy as jnp
from jax import lax
from jax.experimental import pallas as pl
from jax.experimental.pallas import tpu as pltpu
from jax.sharding import PartitionSpec as P

ITERS = 2
RIDGE = 0.5
LANES = 128
F32 = jnp.float32
BF16 = jnp.bfloat16
NT = (((1,), (1,)), ((), ()))
TN = (((0,), (0,)), ((), ()))


def iota(shape, axis):
    return lax.broadcasted_iota(jnp.int32, shape, axis)


def lane_gather(row, index):
    table = jnp.broadcast_to(row, index.shape)
    return jnp.take_along_axis(table, index, axis=1, mode="promise_in_bounds")


def call(body, out_shape, scratch=(), flops=0, size=0):
    return pl.pallas_call(
        body,
        out_shape=out_shape,
        scratch_shapes=list(scratch),
        cost_estimate=pl.CostEstimate(flops=flops, bytes_accessed=size, transcendentals=0),
    )


def route_body(owner_ref, pos_ref, row_ref, lane_ref, hot_ref, place_ref):
    chunks = owner_ref.shape[0]
    sub = iota((LANES, LANES), 0)
    lane = iota((LANES, LANES), 1)
    wide_sub, wide_lane = iota((LANES, 2 * LANES), 0), iota((LANES, 2 * LANES), 1)
    prefix = jnp.where((wide_sub < wide_lane) | (wide_lane >= LANES), 1.0, 0.0).astype(BF16)
    lane_f = lane.astype(F32)

    def step(r, base):
        at = pl.ds(pl.multiple_of(r * LANES, LANES), LANES)
        hot = jnp.where(owner_ref[pl.ds(r, 1), :] == sub, 1.0, 0.0)
        counts = jnp.dot(hot.astype(BF16), prefix, preferred_element_type=F32)
        pos = jnp.sum(hot * (counts[:, :LANES] + base), axis=0, keepdims=True).astype(jnp.int32)
        pos_ref[pl.ds(r, 1), :] = pos
        place_ref[:, at] = jnp.where(pos == sub, 1.0, 0.0).astype(BF16)
        hot_ref[:LANES, at] = (hot * (r + 1).astype(F32)).astype(BF16)
        hot_ref[LANES:, at] = (hot * lane_f).astype(BF16)
        return base + counts[:, LANES:]

    lax.fori_loop(0, chunks, step, jnp.zeros((LANES, LANES), F32), unroll=4)
    held = lax.dot_general(hot_ref[...], place_ref[...], NT, preferred_element_type=F32)
    row_ref[...] = held[:LANES].astype(jnp.int32) - 1
    lane_ref[...] = held[LANES:].astype(jnp.int32)


def route(owner):
    chunks = owner.shape[0]
    rows = chunks * LANES
    plane = jax.ShapeDtypeStruct((LANES, LANES), jnp.int32)
    return call(
        route_body,
        (jax.ShapeDtypeStruct(owner.shape, jnp.int32), plane, plane),
        (pltpu.VMEM((2 * LANES, rows), BF16), pltpu.VMEM((LANES, rows), BF16)),
        flops=2 * 512 * LANES * rows,
        size=rows * 8,
    )(owner)


def place_body(cap, first, *refs):
    if first:
        coef_ref, design_ref, row_ref, lane_ref, slot_ref, weight_ref, mask_ref, pred_ref, pay_ref, vals = refs
        coef = coef_ref[...]
    else:
        coef_ref, upd_ref, design_ref, row_ref, lane_ref, pred_ref, pay_ref, new_ref, vals = refs
        coef = coef_ref[...] + upd_ref[...]
        new_ref[...] = coef
    exps = coef.shape[0]
    rows = design_ref.shape[1]
    chunks = rows // LANES
    width = rows // exps
    per = width // LANES
    maps = coef.astype(BF16)
    for e in range(exps):
        pred = jnp.dot(maps[e], design_ref[:, e * width : (e + 1) * width], preferred_element_type=F32)
        pred_ref[:, e * width : (e + 1) * width] = pred
        for c in range(2):
            for q in range(per):
                r = c * chunks + e * per + q
                vals[r : r + 1, :] = pred[c : c + 1, q * LANES : (q + 1) * LANES]
    if first:
        vals[2 * chunks : 3 * chunks, :] = slot_ref[...].astype(F32)
        for r in range(chunks):
            at = slice(r * LANES, (r + 1) * LANES)
            for k in range(2):
                vals[(3 + k) * chunks + r : (3 + k) * chunks + r + 1, :] = weight_ref[r : r + 1, :] * mask_ref[
                    k : k + 1, at
                ].astype(F32)
    values = 5 if first else 2
    width_out = 4 if first else 2
    lane8 = iota((8, LANES), 1)

    def tile(d, carry):
        at = pl.ds(pl.multiple_of(d * 8, 8), 8)
        source, index = row_ref[at, :], lane_ref[at, :]
        found = [jnp.zeros((8, LANES), F32)] * values
        for r in range(chunks):
            hit = source == r
            for v in range(values):
                got = lane_gather(vals[v * chunks + r : v * chunks + r + 1, :], index)
                found[v] = jnp.where(hit, got, found[v])
        if first:
            spare = LANES - cap
            later = found.pop()
            for v in range(3):
                moved = pltpu.roll(later, (cap - v * spare) % LANES, 1)
                found[v] = jnp.where(lane8 < cap, found[v], moved)
        for v in range(width_out):
            pay_ref[pl.ds(d * 8 * width_out + v, 8, stride=width_out), :] = found[v]
        return carry

    lax.fori_loop(0, LANES // 8, tile, 0)


def place_first(coef, design, row, lane, slot, weight, mask, cap):
    rows = design.shape[1]
    return call(
        functools.partial(place_body, cap, True),
        (jax.ShapeDtypeStruct((2, rows), F32), jax.ShapeDtypeStruct((4 * LANES, LANES), F32)),
        (pltpu.VMEM((5 * rows // LANES, LANES), F32),),
        flops=2 * 16 * design.size,
        size=2 * design.size,
    )(coef, design, row, lane, slot, weight, mask)


def place_next(coef, upd, design, row, lane, cap):
    rows = design.shape[1]
    return call(
        functools.partial(place_body, cap, False),
        (
            jax.ShapeDtypeStruct((2, rows), F32),
            jax.ShapeDtypeStruct((2 * LANES, LANES), F32),
            jax.ShapeDtypeStruct(coef.shape, F32),
        ),
        (pltpu.VMEM((2 * rows // LANES, LANES), F32),),
        flops=2 * 16 * design.size,
        size=2 * design.size,
    )(coef, upd, design, row, lane)


def pieces(x):
    a = x.astype(BF16).astype(F32)
    b = (x - a).astype(BF16).astype(F32)
    c = ((x - a) - b).astype(BF16).astype(F32)
    return (a, b, c)


def owner_body(cap, first, *refs):
    if first:
        pay_ref, ref_ref, prior_ref, ret_ref, id_ref, later_ref, parts = refs
        width = 4
    else:
        pay_ref, ids_in, weights_in, ref_ref, prior_ref, ret_ref, mean_ref, parts = refs
        id_ref, width = ids_in, 2
    lane8 = iota((8, LANES), 1)
    sub8 = iota((8, LANES), 0)
    sub = iota((LANES, LANES), 0)
    spare = LANES - cap

    def split(g, carry):
        def plane(v):
            return pay_ref[pl.ds(g * 8 * width + v, 8, stride=width), :]

        at = pl.ds(pl.multiple_of(g * 8, 8), 8)
        if first:
            p0, p1, ids, weight = plane(0), plane(1), plane(2), plane(3)
            later = jnp.zeros((8, LANES), F32)
            for v, source in enumerate((p0, p1, ids)):
                moved = pltpu.roll(source, (v * spare - cap) % LANES, 1)
                later = jnp.where((lane8 >= v * spare) & (lane8 < (v + 1) * spare), moved, later)
            later_ref[at, :] = later
            weight = jnp.where(lane8 < cap, weight, 0.0)
            id_ref[at, :] = ids.astype(jnp.int32)
        else:
            p0, p1, weight = plane(0), plane(1), weights_in[at, :]
        for v, x in enumerate((weight * p0, weight * p1, weight)):
            for k, piece in enumerate(pieces(x)):
                parts[3 * v + k, at, :] = piece
        return carry

    lax.fori_loop(0, LANES // 8, split, 0)
    group = 8

    def accumulate(g, total):
        left, right = [], []
        for s in range(group):
            src = g * group + s
            ids = id_ref[pl.ds(src, 1), :]
            hit = (ids >> 7) == sub8
            left.append(
                jnp.concatenate(
                    [jnp.where(hit, parts[k, pl.ds(src, 1), :], 0.0) for k in range(9)], axis=0
                ).astype(BF16)
            )
            right.append(jnp.where((ids & 127) == sub, 1.0, 0.0).astype(BF16))
        return total + lax.dot_general(
            jnp.concatenate(left, axis=1), jnp.concatenate(right, axis=1), NT, preferred_element_type=F32
        )

    total = lax.fori_loop(0, LANES // group, accumulate, jnp.zeros((72, LANES), F32))
    sums = [total[24 * v : 24 * v + 8] + total[24 * v + 8 : 24 * v + 16] + total[24 * v + 16 : 24 * v + 24] for v in range(3)]
    rows = prior_ref.shape[0]
    means = [[], []]
    for h in range(rows):
        prior = prior_ref[h : h + 1, :]
        for c in range(2):
            ref = ref_ref[c : c + 1, h * LANES : (h + 1) * LANES]
            mean = (prior * ref + sums[c][h : h + 1]) / (prior + sums[2][h : h + 1])
            means[c].append(mean)
            if not first:
                mean_ref[c : c + 1, h * LANES : (h + 1) * LANES] = mean

    def look(g, carry):
        at = pl.ds(pl.multiple_of(g * 8, 8), 8)
        ids = id_ref[at, :]
        low, high = ids & 127, ids >> 7
        for c in range(2):
            found = jnp.zeros((8, LANES), F32)
            for h in range(rows):
                found = jnp.where(high == h, lane_gather(means[c][h], low), found)
            ret_ref[pl.ds(g * 16 + c, 8, stride=2), :] = found
        return carry

    lax.fori_loop(0, LANES // 8, look, 0)


def owner_first(pay, star_ref, star_prior, cap):
    return call(
        functools.partial(owner_body, cap, True),
        (
            jax.ShapeDtypeStruct((2 * LANES, LANES), F32),
            jax.ShapeDtypeStruct((LANES, LANES), jnp.int32),
            jax.ShapeDtypeStruct((LANES, LANES), F32),
        ),
        (pltpu.VMEM((9, LANES, LANES), F32),),
        flops=2 * 72 * LANES**3,
        size=pay.size * 4,
    )(pay, star_ref, star_prior)


def owner_next(pay, ids, weights, star_ref, star_prior, cap):
    return call(
        functools.partial(owner_body, cap, False),
        (jax.ShapeDtypeStruct((2 * LANES, LANES), F32), jax.ShapeDtypeStruct(star_ref.shape, F32)),
        (pltpu.VMEM((9, LANES, LANES), F32),),
        flops=2 * 72 * LANES**3,
        size=pay.size * 4,
    )(pay, ids, weights, star_ref, star_prior)


def right_body(ret_ref, owner_ref, pos_ref, pred_ref, weighted_ref, right_ref, back):
    chunks = owner_ref.shape[0]
    tiles = chunks // 8
    exps = right_ref.shape[0]
    rows = pred_ref.shape[1]
    width = rows // exps
    owners = [owner_ref[8 * d : 8 * d + 8, :] for d in range(tiles)]
    places = [pos_ref[8 * d : 8 * d + 8, :] for d in range(tiles)]

    def step(o, found):
        found = list(found)
        table = [ret_ref[pl.ds(2 * o + c, 1), :] for c in range(2)]
        for d in range(tiles):
            hit = owners[d] == o
            for c in range(2):
                found[2 * d + c] = jnp.where(hit, lane_gather(table[c], places[d]), found[2 * d + c])
        return tuple(found)

    found = lax.fori_loop(0, LANES, step, (jnp.zeros((8, LANES), F32),) * (2 * tiles), unroll=8)
    for d in range(tiles):
        for c in range(2):
            for s in range(8):
                r = 8 * d + s
                back[c : c + 1, r * LANES : (r + 1) * LANES] = found[2 * d + c][s : s + 1]
    for e in range(exps):
        at = slice(e * width, (e + 1) * width)
        residual = (back[:, at] - pred_ref[:, at]).astype(BF16)
        right_ref[e] = lax.dot_general(residual, weighted_ref[:, at], NT, preferred_element_type=F32)


def right_sides(ret, owner, pos, pred, weighted, exps):
    terms, rows = weighted.shape
    return call(
        right_body,
        jax.ShapeDtypeStruct((exps, 2, terms), F32),
        (pltpu.VMEM((2, rows), F32),),
        flops=2 * 16 * weighted.size,
        size=2 * weighted.size,
    )(ret, owner, pos, pred, weighted)


def gram_body(k, design_ref, weight_ref, mask_ref, gram_ref, weighted_ref):
    terms = design_ref.shape[0]
    rest = terms - LANES
    design = design_ref[...]
    weight = weight_ref[...] * mask_ref[k : k + 1, :].astype(F32)
    weighted = (design.astype(F32) * weight).astype(BF16)
    weighted_ref[...] = weighted
    gram = 0.5 * lax.dot_general(
        jnp.concatenate([weighted, design], axis=1),
        jnp.concatenate([design, weighted], axis=1),
        NT,
        preferred_element_type=F32,
    )
    gram_ref[0, :terms, :] = gram[:, :LANES]
    gram_ref[0, terms:, :] = jnp.zeros((rest, LANES), F32)
    gram_ref[0, terms:, :rest] = gram[LANES:, LANES:]


def gram(design, weight, mask, k, exps):
    terms, rows = design.shape
    width = rows // exps
    packed = 2 * terms - LANES
    return pl.pallas_call(
        functools.partial(gram_body, k),
        grid=(exps,),
        in_specs=[
            pl.BlockSpec((terms, width), lambda e: (0, e)),
            pl.BlockSpec((1, width), lambda e: (0, e)),
            pl.BlockSpec((2, width), lambda e: (0, e)),
        ],
        out_specs=[
            pl.BlockSpec((1, packed, LANES), lambda e: (e, 0, 0)),
            pl.BlockSpec((terms, width), lambda e: (0, e)),
        ],
        out_shape=(jax.ShapeDtypeStruct((exps, packed, LANES), F32), jax.ShapeDtypeStruct(design.shape, BF16)),
        cost_estimate=pl.CostEstimate(
            flops=4 * terms * design.size, bytes_accessed=4 * design.size, transcendentals=0
        ),
    )(design, weight, mask)


def sweep_block(mat, k, tile, terms):
    base = k * 8 - tile * LANES
    sub = iota((8, LANES), 0)
    lane = iota((8, LANES), 1)
    at = pl.ds(pl.multiple_of(k * 8, 8), 8)
    panel = [mat[at, t * LANES : (t + 1) * LANES] for t in range(2)]
    before = list(panel)
    index = jnp.zeros((8, LANES), jnp.int32) + base
    cols = [jnp.take_along_axis(panel[tile], index + j, axis=1, mode="promise_in_bounds") for j in range(8)]
    for j in range(8):
        inverse = 1.0 / jnp.broadcast_to(cols[j][j : j + 1], (8, LANES))
        unit = jnp.where(sub == j, 1.0, 0.0)
        panel[tile] = jnp.where(lane == base + j, unit, panel[tile])
        mine = sub == j

        def sweep(x):
            row = jnp.broadcast_to(x[j : j + 1], (8, LANES)) * inverse
            return jnp.where(mine, row, x - cols[j] * row)

        for m in range(j + 1, 8):
            cols[m] = sweep(cols[m])
        panel = [sweep(x) for x in panel]
    inside = (lane >= base) & (lane < base + 8)
    swept = list(panel)
    swept[tile] = jnp.where(inside, -panel[tile], panel[tile])
    outer = list(panel)
    outer[tile] = jnp.where(inside, 0.0, panel[tile])
    unit = [jnp.zeros((8, LANES), F32)] * 2
    unit[tile] = jnp.where(lane == base + sub, -1.0, 0.0)
    wide = [jnp.concatenate(x, axis=1) for x in (before, outer, unit, swept)]
    r, p, s = pieces(wide[0]), pieces(wide[1]), pieces(wide[1])
    left = jnp.concatenate([r[0], r[0], r[0], r[1], r[1], r[2], s[0], s[1], s[2], s[2] * 0.0], axis=0).astype(BF16)
    right = jnp.concatenate([p[0], p[1], p[2], p[0], p[1], p[0], wide[2], wide[2], wide[2], wide[2] * 0.0], axis=0).astype(BF16)
    change = lax.dot_general(left, right, TN, preferred_element_type=F32)
    keep = jnp.where((iota((1, 2 * LANES), 1) >= k * 8) & (iota((1, 2 * LANES), 1) < k * 8 + 8), 0.0, 1.0)
    mat[...] = mat[...] * keep - change[:terms]
    mat[at, :] = wide[3]


def invert_body(gram_ref, out_ref, mat):
    terms = out_ref.shape[0]
    rest = terms - LANES
    total = gram_ref[0]
    for s in range(1, gram_ref.shape[0]):
        total = total + gram_ref[s]
    square = jnp.concatenate([total[LANES:terms], jnp.zeros((LANES - rest, LANES), F32)], axis=0)
    mat[:, :LANES] = total[:terms]
    mat[:LANES, LANES:] = square.T
    mat[LANES:, LANES:] = total[terms:]
    mat[...] = mat[...] + jnp.where(iota((terms, 2 * LANES), 0) == iota((terms, 2 * LANES), 1), RIDGE, 0.0)

    def first(k, carry):
        sweep_block(mat, k, 0, terms)
        return carry

    def second(k, carry):
        sweep_block(mat, k, 1, terms)
        return carry

    lax.fori_loop(0, LANES // 8, first, 0)
    lax.fori_loop(LANES // 8, terms // 8, second, 0)
    out_ref[...] = -mat[...]


def invert(grams, terms):
    return call(
        invert_body,
        jax.ShapeDtypeStruct((terms, 2 * LANES), F32),
        (pltpu.VMEM((terms, 2 * LANES), F32),),
        flops=2 * 25 * 80 * 256 * 256 * 10,
        size=grams.size * 4,
    )(grams)


def solve_body(right_ref, inverse_ref, out_ref):
    terms = inverse_ref.shape[0]
    right = right_ref[0]
    for s in range(1, right_ref.shape[0]):
        right = right + right_ref[s]
    update = jnp.dot(right, inverse_ref[...], precision=lax.Precision.HIGHEST, preferred_element_type=F32)
    for s in range(right_ref.shape[0]):
        out_ref[s] = update[:, :terms]


def solve(right, inverse):
    return call(solve_body, jax.ShapeDtypeStruct(right.shape, F32), flops=10**6, size=inverse.size * 4)(right, inverse)


def on_device(design, det_weight, outlier_mask, star_owner, star_slot, coef_init, star_ref, star_prior):
    everyone = ("pix", "exp")
    peers = lax.axis_size(everyone)
    terms, rows = design.shape
    exps = coef_init.shape[0]
    cap = 2 * rows // peers
    owner = star_owner.reshape(rows // LANES, LANES)
    slot = star_slot.reshape(rows // LANES, LANES)
    weight_rows = det_weight.reshape(rows // LANES, LANES)
    weight_line = det_weight.reshape(1, rows)
    prior = star_prior.reshape(star_prior.shape[0] // LANES, LANES)

    def exchange(x):
        y = lax.all_to_all(x.reshape(peers, -1, LANES), everyone, split_axis=0, concat_axis=0, tiled=True)
        return y.reshape(x.shape)

    def over_pix(x):
        return lax.all_to_all(x, "pix", split_axis=0, concat_axis=0, tiled=True)

    pos, row, lane = route(owner)
    gram_0, weighted_0 = gram(design, weight_line, outlier_mask, 0, exps)
    gram_1, weighted_1 = gram(design, weight_line, outlier_mask, 1, exps)
    pred, pay = place_first(coef_init, design, row, lane, slot, weight_rows, outlier_mask, cap)
    ret, ids, later = owner_first(exchange(pay), star_ref, prior, cap)
    right = right_sides(exchange(ret), owner, pos, pred, weighted_0, exps)
    inverse_0 = invert(over_pix(gram_0), terms)
    inverse_1 = invert(over_pix(gram_1), terms)
    upd = over_pix(solve(over_pix(right), inverse_0))
    pred, pay, coef = place_next(coef_init, upd, design, row, lane, cap)
    ret, means = owner_next(exchange(pay), ids, later, star_ref, prior, cap)
    right = right_sides(exchange(ret), owner, pos, pred, weighted_1, exps)
    upd = over_pix(solve(over_pix(right), inverse_1))
    return (coef + upd, means)


def solution(mesh):
    placed = (
        P(None, ("pix", "exp")),
        P(("pix", "exp")),
        P(None, ("pix", "exp")),
        P(("pix", "exp"), None),
        P(("pix", "exp")),
        P("exp", None, None),
        P(None, ("pix", "exp")),
        P(("pix", "exp")),
    )
    return jax.shard_map(
        on_device,
        mesh=mesh,
        in_specs=placed,
        out_specs=(P("exp", None, None), P(None, ("pix", "exp"))),
        check_vma=False,
    )
```

```python
import functools

import jax
import jax.numpy as jnp
from jax import lax
from jax.experimental import pallas as pl
from jax.experimental.pallas import tpu as pltpu
from jax.sharding import PartitionSpec as P


RIDGE = 0.5
LANES = 128
F32 = jnp.float32
BF16 = jnp.bfloat16
GRANT = 16 << 20
FLOPS_PER_US = 10**9
NT = (((1,), (1,)), ((), ()))
TN = (((0,), (0,)), ((), ()))


def iota(shape, axis):
    return lax.broadcasted_iota(jnp.int32, shape, axis)


def lane_gather(row, index):
    table = jnp.broadcast_to(row, index.shape)
    return jnp.take_along_axis(table, index, axis=1, mode="promise_in_bounds")


def call(body, out_shape, scratch=(), micros=1, size=0):
    return pl.pallas_call(
        body,
        out_shape=out_shape,
        scratch_shapes=list(scratch),
        compiler_params=pltpu.CompilerParams(vmem_limit_bytes=GRANT),
        cost_estimate=pl.CostEstimate(flops=micros * FLOPS_PER_US, bytes_accessed=size, transcendentals=0),
    )


def route_body(owner_ref, order_ref, row_ref, lane_ref, start_ref, count_ref, line_ref, hot_ref, left_ref, right_ref):
    chunks = owner_ref.shape[0]
    sub = iota((LANES, LANES), 0)
    lane = iota((LANES, LANES), 1)
    wide_sub, wide_lane = iota((LANES, 2 * LANES), 0), iota((LANES, 2 * LANES), 1)
    prefix = jnp.where((wide_sub < wide_lane) | (wide_lane >= LANES), 1.0, 0.0).astype(BF16)

    def rank(r, base):
        at = pl.ds(pl.multiple_of(r * LANES, LANES), LANES)
        hot = jnp.where(owner_ref[pl.ds(r, 1), :] == sub, 1.0, 0.0)
        narrow = hot.astype(BF16)
        hot_ref[:, at] = narrow
        counts = jnp.dot(narrow, prefix, preferred_element_type=F32)
        order_ref[pl.ds(r, 1), :] = jnp.sum(hot * (counts[:, :LANES] + base), axis=0, keepdims=True).astype(jnp.int32)
        return base + counts[:, LANES:]

    counts = lax.fori_loop(0, chunks, rank, jnp.zeros((LANES, LANES), F32), unroll=4)
    high = jnp.floor(counts * (1.0 / LANES))
    split = jnp.concatenate([high, counts - high * LANES], axis=1).astype(BF16)
    below = jnp.where(lane < sub, 1.0, 0.0).astype(BF16)
    starts = jnp.dot(below, split, preferred_element_type=F32)
    start_ref[...] = (starts[:, :LANES] * LANES + starts[:, LANES:]).astype(jnp.int32)
    count_ref[...] = counts.astype(jnp.int32)
    line = jnp.sum(jnp.where(sub < lane, counts, 0.0), axis=0, keepdims=True)
    line8 = jnp.broadcast_to(line, (8, LANES))
    line_ref[...] = line8.astype(jnp.int32)
    high8 = jnp.floor(line8 * (1.0 / LANES))
    first = jnp.where(iota((8, LANES), 0) == 0, high8, line8 - high8 * LANES).astype(BF16)
    begin = jnp.dot(first, hot_ref[...], preferred_element_type=F32)
    sub_rows, lane_line = iota((chunks, LANES), 0), iota((1, LANES), 1).astype(F32)
    for r in range(chunks):
        at = slice(r * LANES, (r + 1) * LANES)
        place = order_ref[r : r + 1, :] + (begin[0:1, at] * LANES + begin[1:2, at]).astype(jnp.int32)
        order_ref[r : r + 1, :] = place
        hit = jnp.where((place >> 7) == sub_rows, 1.0, 0.0)
        left_ref[:chunks, at] = (hit * float(r)).astype(BF16)
        left_ref[chunks:, at] = (hit * lane_line).astype(BF16)
        right_ref[:, at] = jnp.where((place & 127) == sub, 1.0, 0.0).astype(BF16)
    held = lax.dot_general(left_ref[...], right_ref[...], NT, preferred_element_type=F32)
    row_ref[...] = held[:chunks].astype(jnp.int32)
    lane_ref[...] = held[chunks:].astype(jnp.int32)


def route(owner):
    chunks = owner.shape[0]
    rows = chunks * LANES
    line = jax.ShapeDtypeStruct(owner.shape, jnp.int32)
    plane = jax.ShapeDtypeStruct((LANES, LANES), jnp.int32)
    return call(
        route_body,
        (line, line, line, plane, plane, jax.ShapeDtypeStruct((8, LANES), jnp.int32)),
        (pltpu.VMEM((LANES, rows), BF16), pltpu.VMEM((2 * chunks, rows), BF16), pltpu.VMEM((LANES, rows), BF16)),
        micros=4,
        size=rows * 8,
    )(owner)


def pieces(x):
    a = x.astype(BF16).astype(F32)
    b = (x - a).astype(BF16).astype(F32)
    c = ((x - a) - b).astype(BF16).astype(F32)
    return (a, b, c)


def lookup_rows(table, base, chunks, row, lane, values):
    found = [jnp.zeros((8, LANES), F32)] * values
    for r in range(chunks):
        hit = row == r
        for v in range(values):
            at = base[v] + r
            found[v] = jnp.where(hit, lane_gather(table[at : at + 1, :], lane), found[v])
    return found


def place_body(cap, first, *refs):
    if first:
        (coef_ref, design_ref, row_ref, lane_ref, start_ref, count_ref, slot_ref, weight_ref, mask_ref) = refs[:9]
        pred_ref, pay_ref, vals, dense, spread = refs[9:]
        coef = coef_ref[...]
    else:
        coef_ref, upd_ref, design_ref, row_ref, lane_ref, start_ref, count_ref = refs[:7]
        pred_ref, pay_ref, new_ref, vals, dense, spread = refs[7:]
        coef = coef_ref[...] + upd_ref[...]
        new_ref[...] = coef
    exps = coef.shape[0]
    rows = design_ref.shape[1]
    chunks = rows // LANES
    width = rows // exps
    per = width // LANES
    maps = coef.astype(BF16)
    for e in range(exps):
        pred = jnp.dot(maps[e], design_ref[:, e * width : (e + 1) * width], preferred_element_type=F32)
        pred_ref[:, e * width : (e + 1) * width] = pred
        for c in range(2):
            for q in range(per):
                r = c * chunks + e * per + q
                vals[r : r + 1, :] = pred[c : c + 1, q * LANES : (q + 1) * LANES]
    if first:
        vals[2 * chunks : 3 * chunks, :] = slot_ref[...].astype(F32)
        for r in range(chunks):
            at = slice(r * LANES, (r + 1) * LANES)
            for k in range(2):
                vals[(3 + k) * chunks + r : (3 + k) * chunks + r + 1, :] = weight_ref[r : r + 1, :] * mask_ref[
                    k : k + 1, at
                ].astype(F32)
    values = 5 if first else 2
    width_out = 4 if first else 2
    lane8 = iota((8, LANES), 1)

    def gather(d, carry):
        at = pl.ds(pl.multiple_of(d * 8, 8), 8)
        found = lookup_rows(vals, [v * chunks for v in range(values)], chunks, row_ref[at, :], lane_ref[at, :], values)
        for v in range(values):
            for k, piece in enumerate(pieces(found[v])):
                dense[at, (3 * v + k) * LANES : (3 * v + k + 1) * LANES] = piece
        return carry

    lax.fori_loop(0, chunks // 8, gather, 0, unroll=2)
    row_of = start_ref[...] >> 7
    column = iota((LANES, chunks), 1)
    pick = jnp.concatenate(
        [jnp.where(row_of[:, :chunks] + k == column, 1.0, 0.0) for k in range(2)], axis=0
    ).astype(BF16)
    spread[...] = jnp.dot(pick, dense[...].astype(BF16), preferred_element_type=F32)

    def tile(d, carry):
        at = pl.ds(pl.multiple_of(d * 8, 8), 8)
        spot = (start_ref[at, :] & 127) + lane8
        index, near = spot & 127, spot < LANES
        held = lane8 < count_ref[at, :]
        found = []
        for v in range(values):
            rows_of = []
            for k in range(2):
                part = [
                    spread[pl.ds(pl.multiple_of(d * 8 + k * LANES, 8), 8), (3 * v + j) * LANES : (3 * v + j + 1) * LANES]
                    for j in range(3)
                ]
                whole = part[0] + (part[1] + part[2])
                rows_of.append(jnp.take_along_axis(whole, index, axis=1, mode="promise_in_bounds"))
            found.append(jnp.where(held, jnp.where(near, rows_of[0], rows_of[1]), 0.0))
        if first:
            spare = LANES - cap
            later = found.pop()
            for v in range(3):
                moved = pltpu.roll(later, (cap - v * spare) % LANES, 1)
                found[v] = jnp.where(lane8 < cap, found[v], moved)
        for v in range(width_out):
            pay_ref[pl.ds(d * 8 * width_out + v, 8, stride=width_out), :] = found[v]
        return carry

    lax.fori_loop(0, LANES // 8, tile, 0, unroll=2)


def place_scratch(values, chunks):
    return (
        pltpu.VMEM((values * chunks, LANES), F32),
        pltpu.VMEM((chunks, 3 * values * LANES), F32),
        pltpu.VMEM((2 * LANES, 3 * values * LANES), F32),
    )


def place_first(coef, design, row, lane, start, count, slot, weight, mask, cap):
    rows = design.shape[1]
    return call(
        functools.partial(place_body, cap, True),
        (jax.ShapeDtypeStruct((2, rows), F32), jax.ShapeDtypeStruct((4 * LANES, LANES), F32)),
        place_scratch(5, rows // LANES),
        micros=5,
        size=2 * design.size,
    )(coef, design, row, lane, start, count, slot, weight, mask)


def place_next(coef, upd, design, row, lane, start, count, cap):
    rows = design.shape[1]
    return call(
        functools.partial(place_body, cap, False),
        (
            jax.ShapeDtypeStruct((2, rows), F32),
            jax.ShapeDtypeStruct((2 * LANES, LANES), F32),
            jax.ShapeDtypeStruct(coef.shape, F32),
        ),
        place_scratch(2, rows // LANES),
        micros=3,
        size=2 * design.size,
    )(coef, upd, design, row, lane, start, count)


def owner_body(cap, first, *refs):
    if first:
        pay_ref, ref_ref, prior_ref, ret_ref, id_ref, later_ref, parts = refs
        width = 4
    else:
        pay_ref, ids_in, weights_in, ref_ref, prior_ref, ret_ref, mean_ref, parts = refs
        id_ref, width = ids_in, 2
    lane8 = iota((8, LANES), 1)
    sub8 = iota((8, LANES), 0)
    sub = iota((LANES, LANES), 0)
    spare = LANES - cap

    def split(g, carry):
        def plane(v):
            return pay_ref[pl.ds(g * 8 * width + v, 8, stride=width), :]

        at = pl.ds(pl.multiple_of(g * 8, 8), 8)
        if first:
            p0, p1, ids, weight = plane(0), plane(1), plane(2), plane(3)
            later = jnp.zeros((8, LANES), F32)
            for v, source in enumerate((p0, p1, ids)):
                moved = pltpu.roll(source, (v * spare - cap) % LANES, 1)
                later = jnp.where((lane8 >= v * spare) & (lane8 < (v + 1) * spare), moved, later)
            later_ref[at, :] = later
            weight = jnp.where(lane8 < cap, weight, 0.0)
            id_ref[at, :] = ids.astype(jnp.int32)
        else:
            p0, p1, weight = plane(0), plane(1), weights_in[at, :]
        for v, x in enumerate((weight * p0, weight * p1, weight)):
            for k, piece in enumerate(pieces(x)):
                parts[3 * v + k, at, :] = piece
        return carry

    lax.fori_loop(0, LANES // 8, split, 0, unroll=4)
    group = 8

    def accumulate(g, total):
        left, right = [], []
        for s in range(group):
            src = g * group + s
            ids = id_ref[pl.ds(src, 1), :]
            hit = (ids >> 7) == sub8
            left.append(
                jnp.concatenate(
                    [jnp.where(hit, parts[k, pl.ds(src, 1), :], 0.0) for k in range(9)], axis=0
                ).astype(BF16)
            )
            right.append(jnp.where((ids & 127) == sub, 1.0, 0.0).astype(BF16))
        return total + lax.dot_general(
            jnp.concatenate(left, axis=1), jnp.concatenate(right, axis=1), NT, preferred_element_type=F32
        )

    total = lax.fori_loop(0, LANES // group, accumulate, jnp.zeros((72, LANES), F32), unroll=4)
    sums = [total[24 * v : 24 * v + 8] + total[24 * v + 8 : 24 * v + 16] + total[24 * v + 16 : 24 * v + 24] for v in range(3)]
    rows = prior_ref.shape[0]
    means = [[], []]
    for h in range(rows):
        prior = prior_ref[h : h + 1, :]
        for c in range(2):
            ref = ref_ref[c : c + 1, h * LANES : (h + 1) * LANES]
            mean = (prior * ref + sums[c][h : h + 1]) / (prior + sums[2][h : h + 1])
            means[c].append(mean)
            if not first:
                mean_ref[c : c + 1, h * LANES : (h + 1) * LANES] = mean

    def look(g, carry):
        at = pl.ds(pl.multiple_of(g * 8, 8), 8)
        ids = id_ref[at, :]
        low, high = ids & 127, ids >> 7
        for c in range(2):
            found = jnp.zeros((8, LANES), F32)
            for h in range(rows):
                found = jnp.where(high == h, lane_gather(means[c][h], low), found)
            ret_ref[pl.ds(g * 16 + c, 8, stride=2), :] = found
        return carry

    lax.fori_loop(0, LANES // 8, look, 0, unroll=4)


def owner_first(pay, star_ref, star_prior, cap):
    return call(
        functools.partial(owner_body, cap, True),
        (
            jax.ShapeDtypeStruct((2 * LANES, LANES), F32),
            jax.ShapeDtypeStruct((LANES, LANES), jnp.int32),
            jax.ShapeDtypeStruct((LANES, LANES), F32),
        ),
        (pltpu.VMEM((9, LANES, LANES), F32),),
        micros=4,
        size=pay.size * 4,
    )(pay, star_ref, star_prior)


def owner_next(pay, ids, weights, star_ref, star_prior, cap):
    return call(
        functools.partial(owner_body, cap, False),
        (jax.ShapeDtypeStruct((2 * LANES, LANES), F32), jax.ShapeDtypeStruct(star_ref.shape, F32)),
        (pltpu.VMEM((9, LANES, LANES), F32),),
        micros=3,
        size=pay.size * 4,
    )(pay, ids, weights, star_ref, star_prior)


def right_body(step_index, ret_ref, order_ref, start_ref, count_ref, line_ref, pred_ref, design_ref, weight_ref, mask_ref, right_ref, shifted, dense, back, weighted):
    chunks = order_ref.shape[0]
    exps = right_ref.shape[0]
    rows = pred_ref.shape[1]
    width = rows // exps
    lane8 = iota((8, LANES), 1)

    def shift(d, carry):
        at = pl.ds(pl.multiple_of(d * 8, 8), 8)
        offset = start_ref[at, :] & 127
        end = offset + count_ref[at, :]
        index = (lane8 - offset) & 127
        near = (lane8 >= offset) & (lane8 < end)
        far = lane8 + LANES < end
        for c in range(2):
            moved = jnp.take_along_axis(ret_ref[pl.ds(d * 16 + c, 8, stride=2), :], index, axis=1, mode="promise_in_bounds")
            for k, keep in enumerate((near, far)):
                for j, piece in enumerate(pieces(jnp.where(keep, moved, 0.0))):
                    shifted[pl.ds(pl.multiple_of(d * 8 + k * LANES, 8), 8), (3 * c + j) * LANES : (3 * c + j + 1) * LANES] = piece
        return carry

    lax.fori_loop(0, LANES // 8, shift, 0, unroll=4)
    row_of = line_ref[0:1, :] >> 7
    sub_rows = iota((chunks, LANES), 0)
    pick = jnp.concatenate([jnp.where(row_of + k == sub_rows, 1.0, 0.0) for k in range(2)], axis=1).astype(BF16)
    spread = jnp.dot(pick, shifted[...].astype(BF16), preferred_element_type=F32)
    for c in range(2):
        part = [spread[:, (3 * c + j) * LANES : (3 * c + j + 1) * LANES] for j in range(3)]
        dense[c * chunks : (c + 1) * chunks, :] = part[0] + (part[1] + part[2])

    line_weight = weight_ref[...] * mask_ref[step_index : step_index + 1, :].astype(F32)
    for d in range(chunks // 8):
        order = order_ref[8 * d : 8 * d + 8, :]
        found = lookup_rows(dense, [0, chunks], chunks, order >> 7, order & 127, 2)
        for c in range(2):
            for s in range(8):
                r = 8 * d + s
                back[c : c + 1, r * LANES : (r + 1) * LANES] = found[c][s : s + 1]
    for e in range(exps):
        at = slice(e * width, (e + 1) * width)
        weighted = (design_ref[:, at].astype(F32) * line_weight[:, at]).astype(BF16)
        residual = (back[:, at] - pred_ref[:, at]).astype(BF16)
        right_ref[e] = lax.dot_general(residual, weighted, NT, preferred_element_type=F32)


def right_sides(k, ret, order, start, count, line, pred, design, weight, mask, exps):
    terms, rows = design.shape
    chunks = rows // LANES
    return call(
        functools.partial(right_body, k),
        jax.ShapeDtypeStruct((exps, 2, terms), F32),
        (
            pltpu.VMEM((2 * LANES, 6 * LANES), F32),
            pltpu.VMEM((2 * chunks, LANES), F32),
            pltpu.VMEM((2, rows), F32),
            pltpu.VMEM((16, LANES), BF16),
        ),
        micros=2,
        size=2 * design.size,
    )(ret, order, start, count, line, pred, design, weight, mask)


def exposure_gram(k, design_ref, weight_ref, mask_ref):
    design = design_ref[...]
    weight = weight_ref[...] * mask_ref[k : k + 1, :].astype(F32)
    weighted = (design.astype(F32) * weight).astype(BF16)
    return 0.5 * lax.dot_general(
        jnp.concatenate([weighted, design], axis=1),
        jnp.concatenate([design, weighted], axis=1),
        NT,
        preferred_element_type=F32,
    )


def pack(gram, out_ref):
    terms = gram.shape[0]
    rest = terms - LANES
    out_ref[0, :terms, :] = gram[:, :LANES]
    out_ref[0, terms:, :] = jnp.zeros((rest, LANES), F32)
    out_ref[0, terms:, :rest] = gram[LANES:, LANES:]


def gram_body(k, me_ref, design_ref, weight_ref, mask_ref, send_ref, keep_ref):
    gram = exposure_gram(k, design_ref, weight_ref, mask_ref)

    @pl.when(pl.program_id(0) == 0)
    def _():
        pack(gram, send_ref)

    @pl.when(pl.program_id(0) == 1)
    def _():
        pack(gram, keep_ref)


def gram(me, design, weight, mask, k, exps):
    terms, rows = design.shape
    width = rows // exps
    packed = 2 * terms - LANES
    half = exps // 2

    def exposure(s, d, me_ref):
        y = lax.rem(lax.div(me_ref[0], 2) + d, half)
        return 2 * y + lax.rem(me_ref[0] + 1 + s, 2)

    part = jax.ShapeDtypeStruct((half, packed, LANES), F32)
    return pl.pallas_call(
        functools.partial(gram_body, k),
        grid_spec=pltpu.PrefetchScalarGridSpec(
            num_scalar_prefetch=1,
            grid=(2, half),
            in_specs=[
                pl.BlockSpec((terms, width), lambda s, d, me_ref: (0, exposure(s, d, me_ref))),
                pl.BlockSpec((1, width), lambda s, d, me_ref: (0, exposure(s, d, me_ref))),
                pl.BlockSpec((2, width), lambda s, d, me_ref: (0, exposure(s, d, me_ref))),
            ],
            out_specs=[
                pl.BlockSpec((1, packed, LANES), lambda s, d, me_ref: (jnp.where(s == 0, d, half - 1), 0, 0)),
                pl.BlockSpec((1, packed, LANES), lambda s, d, me_ref: (jnp.where(s == 0, 0, d), 0, 0)),
            ],
        ),
        out_shape=(part, part),
        compiler_params=pltpu.CompilerParams(vmem_limit_bytes=GRANT),
        cost_estimate=pl.CostEstimate(
            flops=4 * FLOPS_PER_US, bytes_accessed=4 * design.size, transcendentals=0
        ),
    )(me, design, weight, mask)


def sweep_block(mat, k, tile, terms):
    base = k * 8 - tile * LANES
    sub = iota((8, LANES), 0)
    lane = iota((8, LANES), 1)
    at = pl.ds(pl.multiple_of(k * 8, 8), 8)
    panel = [mat[at, t * LANES : (t + 1) * LANES] for t in range(2)]
    before = list(panel)
    index = jnp.zeros((8, LANES), jnp.int32) + base
    cols = [jnp.take_along_axis(panel[tile], index + j, axis=1, mode="promise_in_bounds") for j in range(8)]
    for j in range(8):
        inverse = 1.0 / jnp.broadcast_to(cols[j][j : j + 1], (8, LANES))
        unit = jnp.where(sub == j, 1.0, 0.0)
        panel[tile] = jnp.where(lane == base + j, unit, panel[tile])
        mine = sub == j

        def sweep(x):
            row = jnp.broadcast_to(x[j : j + 1], (8, LANES)) * inverse
            return jnp.where(mine, row, x - cols[j] * row)

        for m in range(j + 1, 8):
            cols[m] = sweep(cols[m])
        panel = [sweep(x) for x in panel]
    inside = (lane >= base) & (lane < base + 8)
    swept = list(panel)
    swept[tile] = jnp.where(inside, -panel[tile], panel[tile])
    outer = list(panel)
    outer[tile] = jnp.where(inside, 0.0, panel[tile])
    unit = [jnp.zeros((8, LANES), F32)] * 2
    unit[tile] = jnp.where(lane == base + sub, -1.0, 0.0)
    wide = [jnp.concatenate(x, axis=1) for x in (before, outer, unit, swept)]
    r, p, s = pieces(wide[0]), pieces(wide[1]), pieces(wide[1])
    left = jnp.concatenate([r[0], r[0], r[0], r[1], r[1], r[2], s[0], s[1], s[2], s[2] * 0.0], axis=0).astype(BF16)
    right = jnp.concatenate([p[0], p[1], p[2], p[0], p[1], p[0], wide[2], wide[2], wide[2], wide[2] * 0.0], axis=0).astype(BF16)
    change = lax.dot_general(left, right, TN, preferred_element_type=F32)
    keep = jnp.where((iota((1, 2 * LANES), 1) >= k * 8) & (iota((1, 2 * LANES), 1) < k * 8 + 8), 0.0, 1.0)
    mat[...] = mat[...] * keep - change[:terms]
    mat[at, :] = wide[3]


def invert_body(*refs):
    *gram_refs, out_ref, mat = refs
    terms = out_ref.shape[0]
    rest = terms - LANES
    total = functools.reduce(lambda a, b: a + b, [ref[...] for ref in gram_refs])
    square = jnp.concatenate([total[LANES:terms], jnp.zeros((LANES - rest, LANES), F32)], axis=0)
    mat[:, :LANES] = total[:terms]
    mat[:LANES, LANES:] = square.T
    mat[LANES:, LANES:] = total[terms:]
    mat[...] = mat[...] + jnp.where(iota((terms, 2 * LANES), 0) == iota((terms, 2 * LANES), 1), RIDGE, 0.0)

    def first(k, carry):
        sweep_block(mat, k, 0, terms)
        return carry

    def second(k, carry):
        sweep_block(mat, k, 1, terms)
        return carry

    lax.fori_loop(0, LANES // 8, first, 0)
    lax.fori_loop(LANES // 8, terms // 8, second, 0)
    out_ref[...] = -mat[...]


def invert(grams, terms):
    return call(
        invert_body,
        jax.ShapeDtypeStruct((terms, 2 * LANES), F32),
        (pltpu.VMEM((terms, 2 * LANES), F32),),
        micros=10,
        size=4 * len(grams) * grams[0].size,
    )(*grams)


def solve_body(right_ref, inverse_ref, out_ref):
    terms = inverse_ref.shape[0]
    right = right_ref[0]
    for s in range(1, right_ref.shape[0]):
        right = right + right_ref[s]
    update = jnp.dot(right, inverse_ref[...], precision=lax.Precision.HIGHEST, preferred_element_type=F32)
    for s in range(right_ref.shape[0]):
        out_ref[s] = update[:, :terms]


def solve(right, inverse):
    return call(solve_body, jax.ShapeDtypeStruct(right.shape, F32), micros=1, size=inverse.size * 4)(right, inverse)


def on_device(design, det_weight, outlier_mask, star_owner, star_slot, coef_init, star_ref, star_prior):
    everyone = ("pix", "exp")
    peers = lax.axis_size(everyone)
    terms, rows = design.shape
    exps = coef_init.shape[0]
    cap = 2 * rows // peers
    owner = star_owner.reshape(rows // LANES, LANES)
    slot = star_slot.reshape(rows // LANES, LANES)
    weight_rows = det_weight.reshape(rows // LANES, LANES)
    weight_line = det_weight.reshape(1, rows)
    prior = star_prior.reshape(star_prior.shape[0] // LANES, LANES)

    def exchange(x):
        y = lax.all_to_all(x.reshape(peers, -1, LANES), everyone, split_axis=0, concat_axis=0, tiled=True)
        return y.reshape(x.shape)

    def over_pix(x):
        return lax.all_to_all(x, "pix", split_axis=0, concat_axis=0, tiled=True)

    pixes = lax.axis_size("pix")
    me = lax.axis_index("pix").reshape(1)

    def norm_exchange(send, keep):
        got = lax.ppermute(send, "pix", [(i, i ^ 1) for i in range(pixes)])
        parts = []
        for d in range(pixes // 2):
            part = keep[d] + got[d]
            if d > 0:
                part = lax.ppermute(part, "pix", [(i, (i + 2 * d) % pixes) for i in range(pixes)])
            parts.append(part)
        return parts

    order, row, lane, start, count, line = route(owner)
    pred, pay = place_first(coef_init, design, row, lane, start, count, slot, weight_rows, outlier_mask, cap)
    pay = exchange(pay)
    send, keep = gram(me, design, weight_line, outlier_mask, 0, exps)
    gram_0 = norm_exchange(send, keep)
    ret, ids, later = owner_first(pay, star_ref, prior, cap)
    ret = exchange(ret)
    inverse_0 = invert(gram_0, terms)
    right = right_sides(0, ret, order, start, count, line, pred, design, weight_line, outlier_mask, exps)
    right = over_pix(right)
    send, keep = gram(me, design, weight_line, outlier_mask, 1, exps)
    gram_1 = norm_exchange(send, keep)
    upd = solve(right, inverse_0)
    upd = over_pix(upd)
    pred, pay, coef = place_next(coef_init, upd, design, row, lane, start, count, cap)
    pay = exchange(pay)
    ret, means = owner_next(pay, ids, later, star_ref, prior, cap)
    ret = exchange(ret)
    inverse_1 = invert(gram_1, terms)
    right = right_sides(1, ret, order, start, count, line, pred, design, weight_line, outlier_mask, exps)
    right = over_pix(right)
    upd = solve(right, inverse_1)
    upd = over_pix(upd)
    return (coef + upd, means)


def solution(mesh):
    placed = (
        P(None, ("pix", "exp")),
        P(("pix", "exp")),
        P(None, ("pix", "exp")),
        P(("pix", "exp"), None),
        P(("pix", "exp")),
        P("exp", None, None),
        P(None, ("pix", "exp")),
        P(("pix", "exp")),
    )
    return jax.shard_map(
        on_device,
        mesh=mesh,
        in_specs=placed,
        out_specs=(P("exp", None, None), P(None, ("pix", "exp"))),
        check_vma=False,
    )
```

```python
import functools

import jax
import jax.numpy as jnp
from jax import lax
from jax.experimental import pallas as pl
from jax.experimental.pallas import tpu as pltpu
from jax.sharding import PartitionSpec as P


RIDGE = 0.5
LANES = 128
F32 = jnp.float32
BF16 = jnp.bfloat16
GRANT = 16 << 20
FLOPS_PER_US = 10**9
SPLIT = 11
NT = (((1,), (1,)), ((), ()))
TN = (((0,), (0,)), ((), ()))


def iota(shape, axis):
    return lax.broadcasted_iota(jnp.int32, shape, axis)


def lane_gather(row, index):
    table = jnp.broadcast_to(row, index.shape)
    return jnp.take_along_axis(table, index, axis=1, mode="promise_in_bounds")


def call(body, out_shape, scratch=(), micros=1, size=0, in_specs=None):
    specs = {} if in_specs is None else {"in_specs": in_specs}
    return pl.pallas_call(
        body,
        **specs,
        out_shape=out_shape,
        scratch_shapes=list(scratch),
        compiler_params=pltpu.CompilerParams(vmem_limit_bytes=GRANT),
        cost_estimate=pl.CostEstimate(flops=micros * FLOPS_PER_US, bytes_accessed=size, transcendentals=0),
    )


def route_body(owner_ref, order_ref, row_ref, lane_ref, start_ref, count_ref, line_ref, hot_ref, left_ref, right_ref):
    chunks = owner_ref.shape[0]
    sub = iota((LANES, LANES), 0)
    lane = iota((LANES, LANES), 1)
    wide_sub, wide_lane = iota((LANES, 2 * LANES), 0), iota((LANES, 2 * LANES), 1)
    prefix = jnp.where((wide_sub < wide_lane) | (wide_lane >= LANES), 1.0, 0.0).astype(BF16)

    def rank(r, base):
        at = pl.ds(pl.multiple_of(r * LANES, LANES), LANES)
        hot = jnp.where(owner_ref[pl.ds(r, 1), :] == sub, 1.0, 0.0)
        narrow = hot.astype(BF16)
        hot_ref[:, at] = narrow
        counts = jnp.dot(narrow, prefix, preferred_element_type=F32)
        order_ref[pl.ds(r, 1), :] = jnp.sum(hot * (counts[:, :LANES] + base), axis=0, keepdims=True).astype(jnp.int32)
        return base + counts[:, LANES:]

    counts = lax.fori_loop(0, chunks, rank, jnp.zeros((LANES, LANES), F32), unroll=8)
    high = jnp.floor(counts * (1.0 / LANES))
    split = jnp.concatenate([high, counts - high * LANES], axis=1).astype(BF16)
    below = jnp.where(lane < sub, 1.0, 0.0).astype(BF16)
    starts = jnp.dot(below, split, preferred_element_type=F32)
    start_ref[...] = (starts[:, :LANES] * LANES + starts[:, LANES:]).astype(jnp.int32)
    count_ref[...] = counts.astype(jnp.int32)
    line = jnp.sum(jnp.where(sub < lane, counts, 0.0), axis=0, keepdims=True)
    line8 = jnp.broadcast_to(line, (8, LANES))
    line_ref[...] = line8.astype(jnp.int32)
    high8 = jnp.floor(line8 * (1.0 / LANES))
    first = jnp.where(iota((8, LANES), 0) == 0, high8, line8 - high8 * LANES).astype(BF16)
    begin = jnp.dot(first, hot_ref[...], preferred_element_type=F32)
    sub_rows, lane_line = iota((chunks, LANES), 0), iota((1, LANES), 1).astype(F32)
    for r in range(chunks):
        at = slice(r * LANES, (r + 1) * LANES)
        place = order_ref[r : r + 1, :] + (begin[0:1, at] * LANES + begin[1:2, at]).astype(jnp.int32)
        order_ref[r : r + 1, :] = place
        hit = jnp.where((place >> 7) == sub_rows, 1.0, 0.0)
        left_ref[:chunks, at] = (hit * float(r)).astype(BF16)
        left_ref[chunks:, at] = (hit * lane_line).astype(BF16)
        right_ref[:, at] = jnp.where((place & 127) == sub, 1.0, 0.0).astype(BF16)
    held = lax.dot_general(left_ref[...], right_ref[...], NT, preferred_element_type=F32)
    row_ref[...] = held[:chunks].astype(jnp.int32)
    lane_ref[...] = held[chunks:].astype(jnp.int32)


def route(owner):
    chunks = owner.shape[0]
    rows = chunks * LANES
    line = jax.ShapeDtypeStruct(owner.shape, jnp.int32)
    plane = jax.ShapeDtypeStruct((LANES, LANES), jnp.int32)
    return call(
        route_body,
        (line, line, line, plane, plane, jax.ShapeDtypeStruct((8, LANES), jnp.int32)),
        (pltpu.VMEM((LANES, rows), BF16), pltpu.VMEM((2 * chunks, rows), BF16), pltpu.VMEM((LANES, rows), BF16)),
        micros=4,
        size=rows * 8,
    )(owner)


def pieces(x):
    a = x.astype(BF16).astype(F32)
    b = (x - a).astype(BF16).astype(F32)
    c = ((x - a) - b).astype(BF16).astype(F32)
    return (a, b, c)


def lookup_rows(table, base, chunks, row, lane, values):
    found = [jnp.zeros((8, LANES), F32)] * values
    for r in range(chunks):
        hit = row == r
        for v in range(values):
            at = base[v] + r
            found[v] = jnp.where(hit, lane_gather(table[at : at + 1, :], lane), found[v])
    return found


def place_body(cap, first, *refs):
    if first:
        (coef_ref, design_ref, row_ref, lane_ref, start_ref, count_ref, slot_ref, weight_ref, mask_ref) = refs[:9]
        pred_ref, pay_ref, vals, dense, spread = refs[9:]
        coef = coef_ref[...]
    else:
        coef_ref, upd_ref, design_ref, row_ref, lane_ref, start_ref, count_ref = refs[:7]
        pred_ref, pay_ref, new_ref, vals, dense, spread = refs[7:]
        coef = coef_ref[...] + upd_ref[...]
        new_ref[...] = coef
    exps = coef.shape[0]
    rows = design_ref.shape[1]
    chunks = rows // LANES
    width = rows // exps
    per = width // LANES
    maps = coef.astype(BF16)
    for e in range(exps):
        pred = jnp.dot(maps[e], design_ref[:, e * width : (e + 1) * width], preferred_element_type=F32)
        pred_ref[:, e * width : (e + 1) * width] = pred
        for c in range(2):
            for q in range(per):
                r = c * chunks + e * per + q
                vals[r : r + 1, :] = pred[c : c + 1, q * LANES : (q + 1) * LANES]
    if first:
        vals[2 * chunks : 3 * chunks, :] = slot_ref[...].astype(F32)
        for r in range(chunks):
            at = slice(r * LANES, (r + 1) * LANES)
            for k in range(2):
                vals[(3 + k) * chunks + r : (3 + k) * chunks + r + 1, :] = weight_ref[r : r + 1, :] * mask_ref[
                    k : k + 1, at
                ].astype(F32)
    values = 5 if first else 2
    width_out = 4 if first else 2
    lane8 = iota((8, LANES), 1)

    def gather(d, carry):
        at = pl.ds(pl.multiple_of(d * 8, 8), 8)
        found = lookup_rows(vals, [v * chunks for v in range(values)], chunks, row_ref[at, :], lane_ref[at, :], values)
        for v in range(values):
            for k, piece in enumerate(pieces(found[v])):
                dense[at, (3 * v + k) * LANES : (3 * v + k + 1) * LANES] = piece
        return carry

    lax.fori_loop(0, chunks // 8, gather, 0, unroll=2)
    row_of = start_ref[...] >> 7
    column = iota((LANES, chunks), 1)
    pick = jnp.concatenate(
        [jnp.where(row_of[:, :chunks] + k == column, 1.0, 0.0) for k in range(2)], axis=0
    ).astype(BF16)
    spread[...] = jnp.dot(pick, dense[...].astype(BF16), preferred_element_type=F32)

    def tile(d, carry):
        at = pl.ds(pl.multiple_of(d * 8, 8), 8)
        spot = (start_ref[at, :] & 127) + lane8
        index, near = spot & 127, spot < LANES
        held = lane8 < count_ref[at, :]
        found = []
        for v in range(values):
            rows_of = []
            for k in range(2):
                part = [
                    spread[pl.ds(pl.multiple_of(d * 8 + k * LANES, 8), 8), (3 * v + j) * LANES : (3 * v + j + 1) * LANES]
                    for j in range(3)
                ]
                whole = part[0] + (part[1] + part[2])
                rows_of.append(jnp.take_along_axis(whole, index, axis=1, mode="promise_in_bounds"))
            found.append(jnp.where(held, jnp.where(near, rows_of[0], rows_of[1]), 0.0))
        if first:
            spare = LANES - cap
            later = found.pop()
            for v in range(3):
                moved = pltpu.roll(later, (cap - v * spare) % LANES, 1)
                found[v] = jnp.where(lane8 < cap, found[v], moved)
        for v in range(width_out):
            pay_ref[pl.ds(d * 8 * width_out + v, 8, stride=width_out), :] = found[v]
        return carry

    lax.fori_loop(0, LANES // 8, tile, 0, unroll=2)


def place_scratch(values, chunks):
    return (
        pltpu.VMEM((values * chunks, LANES), F32),
        pltpu.VMEM((chunks, 3 * values * LANES), F32),
        pltpu.VMEM((2 * LANES, 3 * values * LANES), F32),
    )


def place_first(coef, design, row, lane, start, count, slot, weight, mask, cap):
    rows = design.shape[1]
    return call(
        functools.partial(place_body, cap, True),
        (pltpu.HBM((2, rows), F32), jax.ShapeDtypeStruct((4 * LANES, LANES), F32)),
        place_scratch(5, rows // LANES),
        micros=5,
        size=2 * design.size,
    )(coef, design, row, lane, start, count, slot, weight, mask)


def place_next(coef, upd, design, row, lane, start, count, cap):
    rows = design.shape[1]
    return call(
        functools.partial(place_body, cap, False),
        (
            pltpu.HBM((2, rows), F32),
            jax.ShapeDtypeStruct((2 * LANES, LANES), F32),
            jax.ShapeDtypeStruct(coef.shape, F32),
        ),
        place_scratch(2, rows // LANES),
        micros=3,
        size=2 * design.size,
    )(coef, upd, design, row, lane, start, count)


def owner_body(cap, first, *refs):
    if first:
        pay_ref, ref_ref, prior_ref, ret_ref, kept_ref, parts, id_ref = refs
        width = 4
    else:
        pay_ref, kept_ref, ref_ref, prior_ref, ret_ref, mean_ref, parts, id_ref = refs
        width = 2
    lane8 = iota((8, LANES), 1)
    sub8 = iota((8, LANES), 0)
    sub = iota((LANES, LANES), 0)
    spare = LANES - cap

    def split(g, carry):
        def plane(v):
            return pay_ref[pl.ds(g * 8 * width + v, 8, stride=width), :]

        at = pl.ds(pl.multiple_of(g * 8, 8), 8)
        if first:
            p0, p1, ids, weight = plane(0), plane(1), plane(2), plane(3)
            later = jnp.zeros((8, LANES), F32)
            for v, source in enumerate((p0, p1, ids)):
                moved = pltpu.roll(source, (v * spare - cap) % LANES, 1)
                later = jnp.where((lane8 >= v * spare) & (lane8 < (v + 1) * spare), moved, later)
            kept_ref[0, at, :] = ids
            kept_ref[1, at, :] = later
            weight = jnp.where(lane8 < cap, weight, 0.0)
            id_ref[at, :] = ids.astype(jnp.int32)
        else:
            p0, p1, weight = plane(0), plane(1), kept_ref[1, at, :]
            id_ref[at, :] = kept_ref[0, at, :].astype(jnp.int32)
        for v, x in enumerate((weight * p0, weight * p1, weight)):
            for k, piece in enumerate(pieces(x)):
                parts[3 * v + k, at, :] = piece
        return carry

    lax.fori_loop(0, LANES // 8, split, 0, unroll=4)
    group = 8

    def accumulate(g, total):
        left, right = [], []
        for s in range(group):
            src = g * group + s
            ids = id_ref[pl.ds(src, 1), :]
            hit = (ids >> 7) == sub8
            left.append(
                jnp.concatenate(
                    [jnp.where(hit, parts[k, pl.ds(src, 1), :], 0.0) for k in range(9)], axis=0
                ).astype(BF16)
            )
            right.append(jnp.where((ids & 127) == sub, 1.0, 0.0).astype(BF16))
        return total + lax.dot_general(
            jnp.concatenate(left, axis=1), jnp.concatenate(right, axis=1), NT, preferred_element_type=F32
        )

    total = lax.fori_loop(0, LANES // group, accumulate, jnp.zeros((72, LANES), F32), unroll=4)
    sums = [total[24 * v : 24 * v + 8] + total[24 * v + 8 : 24 * v + 16] + total[24 * v + 16 : 24 * v + 24] for v in range(3)]
    rows = prior_ref.shape[0]
    means = [[], []]
    for h in range(rows):
        prior = prior_ref[h : h + 1, :]
        for c in range(2):
            ref = ref_ref[c : c + 1, h * LANES : (h + 1) * LANES]
            mean = (prior * ref + sums[c][h : h + 1]) / (prior + sums[2][h : h + 1])
            means[c].append(mean)
            if not first:
                mean_ref[c : c + 1, h * LANES : (h + 1) * LANES] = mean

    def look(g, carry):
        at = pl.ds(pl.multiple_of(g * 8, 8), 8)
        ids = id_ref[at, :]
        low, high = ids & 127, ids >> 7
        for c in range(2):
            found = jnp.zeros((8, LANES), F32)
            for h in range(rows):
                found = jnp.where(high == h, lane_gather(means[c][h], low), found)
            ret_ref[pl.ds(g * 16 + c, 8, stride=2), :] = found
        return carry

    lax.fori_loop(0, LANES // 8, look, 0, unroll=4)


def owner_first(pay, star_ref, star_prior, cap):
    return call(
        functools.partial(owner_body, cap, True),
        (
            jax.ShapeDtypeStruct((2 * LANES, LANES), F32),
            pltpu.HBM((2, LANES, LANES), F32),
        ),
        (pltpu.VMEM((9, LANES, LANES), F32), pltpu.VMEM((LANES, LANES), jnp.int32)),
        micros=4,
        size=pay.size * 4,
    )(pay, star_ref, star_prior)


def owner_next(pay, kept, star_ref, star_prior, cap):
    return call(
        functools.partial(owner_body, cap, False),
        (jax.ShapeDtypeStruct((2 * LANES, LANES), F32), jax.ShapeDtypeStruct(star_ref.shape, F32)),
        (
            pltpu.VMEM((9, LANES, LANES), F32),
            pltpu.VMEM((LANES, LANES), jnp.int32),
        ),
        micros=3,
        size=pay.size * 4,
    )(pay, kept, star_ref, star_prior)


def right_body(step_index, *refs):
    ret_ref, order_ref, start_ref, count_ref, line_ref, pred_ref, design_ref, weight_ref, mask_ref = refs[:9]
    right_ref, shifted, dense, back = refs[9:]
    chunks = order_ref.shape[0]
    exps = right_ref.shape[0]
    rows = pred_ref.shape[1]
    width = rows // exps
    lane8 = iota((8, LANES), 1)

    def shift(d, carry):
        at = pl.ds(pl.multiple_of(d * 8, 8), 8)
        offset = start_ref[at, :] & 127
        end = offset + count_ref[at, :]
        index = (lane8 - offset) & 127
        near = (lane8 >= offset) & (lane8 < end)
        far = lane8 + LANES < end
        for c in range(2):
            moved = jnp.take_along_axis(ret_ref[pl.ds(d * 16 + c, 8, stride=2), :], index, axis=1, mode="promise_in_bounds")
            for k, keep in enumerate((near, far)):
                for j, piece in enumerate(pieces(jnp.where(keep, moved, 0.0))):
                    shifted[pl.ds(pl.multiple_of(d * 8 + k * LANES, 8), 8), (3 * c + j) * LANES : (3 * c + j + 1) * LANES] = piece
        return carry

    lax.fori_loop(0, LANES // 8, shift, 0, unroll=4)
    row_of = line_ref[0:1, :] >> 7
    sub_rows = iota((chunks, LANES), 0)
    pick = jnp.concatenate([jnp.where(row_of + k == sub_rows, 1.0, 0.0) for k in range(2)], axis=1).astype(BF16)
    spread = jnp.dot(pick, shifted[...].astype(BF16), preferred_element_type=F32)
    for c in range(2):
        part = [spread[:, (3 * c + j) * LANES : (3 * c + j + 1) * LANES] for j in range(3)]
        dense[c * chunks : (c + 1) * chunks, :] = part[0] + (part[1] + part[2])

    line_weight = weight_ref[...] * mask_ref[step_index : step_index + 1, :].astype(F32)
    for d in range(chunks // 8):
        order = order_ref[8 * d : 8 * d + 8, :]
        found = lookup_rows(dense, [0, chunks], chunks, order >> 7, order & 127, 2)
        for c in range(2):
            for s in range(8):
                r = 8 * d + s
                back[c : c + 1, r * LANES : (r + 1) * LANES] = found[c][s : s + 1]
    for e in range(exps):
        at = slice(e * width, (e + 1) * width)
        weighted = (design_ref[:, at].astype(F32) * line_weight[:, at]).astype(BF16)
        residual = (back[:, at] - pred_ref[:, at]).astype(BF16)
        right_ref[e] = lax.dot_general(residual, weighted, NT, preferred_element_type=F32)


def right_sides(k, ret, order, start, count, line, pred, design, weight, mask, exps):
    terms, rows = design.shape
    chunks = rows // LANES
    return call(
        functools.partial(right_body, k),
        jax.ShapeDtypeStruct((exps, 2, terms), F32),
        (
            pltpu.VMEM((2 * LANES, 6 * LANES), F32),
            pltpu.VMEM((2 * chunks, LANES), F32),
            pltpu.VMEM((2, rows), F32),
        ),
        micros=2,
        size=2 * design.size,
    )(ret, order, start, count, line, pred, design, weight, mask)


def exposure_gram(k, design_ref, weight_ref, mask_ref):
    design = design_ref[...]
    weight = weight_ref[...] * mask_ref[k : k + 1, :].astype(F32)
    weighted = (design.astype(F32) * weight).astype(BF16)
    return 0.5 * lax.dot_general(
        jnp.concatenate([weighted, design], axis=1),
        jnp.concatenate([design, weighted], axis=1),
        NT,
        preferred_element_type=F32,
    )


def pack(gram, out_ref):
    terms = gram.shape[0]
    rest = terms - LANES
    out_ref[0, :terms, :] = gram[:, :LANES]
    out_ref[0, terms:, :] = jnp.zeros((rest, LANES), F32)
    out_ref[0, terms:, :rest] = gram[LANES:, LANES:]


def gram_body(k, me_ref, design_ref, weight_ref, mask_ref, gram_ref):
    pack(exposure_gram(k, design_ref, weight_ref, mask_ref), gram_ref)


def gram(me, design, weight, mask, k, exps, mine):
    terms, rows = design.shape
    width = rows // exps
    packed = 2 * terms - LANES
    half = exps // 2

    def exposure(d, me_ref):
        return 2 * lax.rem(lax.div(me_ref[0], 2) + d, half) + lax.rem(me_ref[0] + (0 if mine else 1), 2)

    return pl.pallas_call(
        functools.partial(gram_body, k),
        grid_spec=pltpu.PrefetchScalarGridSpec(
            num_scalar_prefetch=1,
            grid=(half,),
            in_specs=[
                pl.BlockSpec((terms, width), lambda d, me_ref: (0, exposure(d, me_ref))),
                pl.BlockSpec((1, width), lambda d, me_ref: (0, exposure(d, me_ref))),
                pl.BlockSpec((2, width), lambda d, me_ref: (0, exposure(d, me_ref))),
            ],
            out_specs=pl.BlockSpec((1, packed, LANES), lambda d, me_ref: (d, 0, 0)),
        ),
        out_shape=jax.ShapeDtypeStruct((half, packed, LANES), F32),
        compiler_params=pltpu.CompilerParams(vmem_limit_bytes=GRANT),
        cost_estimate=pl.CostEstimate(
            flops=2 * FLOPS_PER_US, bytes_accessed=2 * design.size, transcendentals=0
        ),
    )(me, design, weight, mask)


def eliminate(panel, base, tile):
    sub = iota((8, LANES), 0)
    lane = iota((8, LANES), 1)
    panel = list(panel)
    index = jnp.zeros((8, LANES), jnp.int32) + base
    cols = [jnp.take_along_axis(panel[tile], index + j, axis=1, mode="promise_in_bounds") for j in range(8)]
    for j in range(8):
        inverse = 1.0 / jnp.broadcast_to(cols[j][j : j + 1], (8, LANES))
        mine = sub == j
        panel[tile] = jnp.where(lane == base + j, jnp.where(mine, 1.0, 0.0), panel[tile])

        def sweep(x):
            row = jnp.broadcast_to(x[j : j + 1], (8, LANES)) * inverse
            return jnp.where(mine, row, x - cols[j] * row)

        for m in range(j + 1, 8):
            cols[m] = sweep(cols[m])
        panel = [sweep(x) for x in panel]
    inside = (lane >= base) & (lane < base + 8)
    panel[tile] = jnp.where(inside, -panel[tile], panel[tile])
    return panel


def outside(k, rows):
    lane = iota((rows, 2 * LANES), 1)
    return jnp.where((lane >= k * 8) & (lane < k * 8 + 8), 0.0, 1.0)


def block_rows(k):
    return pl.ds(pl.multiple_of(k * 8, 8), 8)


def update_all(mat, k, before, swept):
    r, q = pieces(jnp.concatenate(before, axis=1)), pieces(jnp.concatenate(swept, axis=1))
    left = jnp.concatenate([r[0], r[0], r[0], r[1], r[1], r[2]], axis=0).astype(BF16)
    right = jnp.concatenate([q[0], q[1], q[2], q[0], q[1], q[0]], axis=0).astype(BF16)
    change = lax.dot_general(left, right, TN, preferred_element_type=F32)
    mat[...] = mat[...] * outside(k, 1) - change[: mat.shape[0]]
    mat[block_rows(k), :] = jnp.concatenate(swept, axis=1)


def update_next(mat, k, swept, base, tile):
    at = block_rows(jnp.minimum(k + 1, mat.shape[0] // 8 - 1))
    rows = [mat[at, t * LANES : (t + 1) * LANES] for t in range(2)]
    keep = outside(k, 8)
    index = jnp.zeros((8, LANES), jnp.int32) + base
    fresh = [rows[t] * keep[:, t * LANES : (t + 1) * LANES] for t in range(2)]
    for j in range(8):
        col = jnp.take_along_axis(rows[tile], index + j, axis=1, mode="promise_in_bounds")
        fresh = [fresh[t] - col * jnp.broadcast_to(swept[t][j : j + 1], (8, LANES)) for t in range(2)]
    return fresh


def sweep_range(mat, low, high):
    start = low // 16
    base = low * 8 - start * LANES
    first = [mat[low * 8 : low * 8 + 8, t * LANES : (t + 1) * LANES] for t in range(2)]
    swept = eliminate(first, base, start)
    carry = (tuple(first), tuple(swept), tuple(update_next(mat, low, swept, base, start)))
    for tile in range(2):
        begin, end = max(low + 1, 16 * tile), min(high, 16 * (tile + 1))

        def step(k, carry):
            before, swept, panel = carry
            base = k * 8 - tile * LANES
            fresh = eliminate(panel, base, tile)
            update_all(mat, k - 1, before, swept)
            return (panel, tuple(fresh), tuple(update_next(mat, k, fresh, base, tile)))

        if begin < end:
            carry = lax.fori_loop(begin, end, step, carry)
    update_all(mat, high - 1, carry[0], carry[1])


def unpack(gram_refs, mat):
    terms = mat.shape[0]
    rest = terms - LANES
    total = functools.reduce(lambda a, b: a + b, [ref[...] for ref in gram_refs])
    square = jnp.concatenate([total[LANES:terms], jnp.zeros((LANES - rest, LANES), F32)], axis=0)
    mat[:, :LANES] = total[:terms]
    mat[:LANES, LANES:] = square.T
    mat[LANES:, LANES:] = total[terms:]
    mat[...] = mat[...] + jnp.where(iota((terms, 2 * LANES), 0) == iota((terms, 2 * LANES), 1), RIDGE, 0.0)


def invert_body(*refs):
    *gram_refs, out_ref, mat = refs
    unpack(gram_refs, mat)
    sweep_range(mat, 0, mat.shape[0] // 8)
    out_ref[...] = -mat[...]


def invert(grams, terms):
    return call(
        invert_body,
        pltpu.HBM((terms, 2 * LANES), F32),
        (pltpu.VMEM((terms, 2 * LANES), F32),),
        micros=8,
        size=4 * len(grams) * grams[0].size,
    )(*grams)


def invert_first_body(high, *refs):
    *gram_refs, mat = refs
    unpack(gram_refs, mat)
    sweep_range(mat, 0, high)


def invert_rest_body(low, part_ref, out_ref):
    out_ref[...] = part_ref[...]
    sweep_range(out_ref, low, out_ref.shape[0] // 8)
    out_ref[...] = -out_ref[...]


def invert_first(grams, terms, high):
    return call(
        functools.partial(invert_first_body, high),
        jax.ShapeDtypeStruct((terms, 2 * LANES), F32),
        micros=4,
        size=4 * len(grams) * grams[0].size,
    )(*grams)


def invert_rest(part, low):
    return call(
        functools.partial(invert_rest_body, low),
        jax.ShapeDtypeStruct(part.shape, F32),
        micros=4,
        size=8 * part.size,
    )(part)


def solve_body(last, *refs):
    if last:
        me_ref, coef_ref, right_ref, inverse_ref, out_ref = refs
    else:
        right_ref, inverse_ref, out_ref = refs
    terms = inverse_ref.shape[0]
    right = right_ref[0]
    for s in range(1, right_ref.shape[0]):
        right = right + right_ref[s]
    update = jnp.dot(right, inverse_ref[...], precision=lax.Precision.HIGHEST, preferred_element_type=F32)[:, :terms]
    if last:
        update = coef_ref[me_ref[0]] + update
    for s in range(right_ref.shape[0]):
        out_ref[s] = update


def solve(right, inverse):
    shape = jax.ShapeDtypeStruct(right.shape, F32)
    return call(functools.partial(solve_body, False), shape, micros=1, size=inverse.size * 4)(right, inverse)


def solve_last(me, coef, right, inverse):
    shape = jax.ShapeDtypeStruct(right.shape, F32)
    specs = [pl.BlockSpec(memory_space=pltpu.SMEM)] + [pl.BlockSpec()] * 3
    return call(functools.partial(solve_body, True), shape, micros=1, size=inverse.size * 4, in_specs=specs)(
        me, coef, right, inverse
    )


def on_device(design, det_weight, outlier_mask, star_owner, star_slot, coef_init, star_ref, star_prior):
    everyone = ("pix", "exp")
    peers = lax.axis_size(everyone)
    terms, rows = design.shape
    exps = coef_init.shape[0]
    cap = 2 * rows // peers
    owner = star_owner.reshape(rows // LANES, LANES)
    slot = star_slot.reshape(rows // LANES, LANES)
    weight_rows = det_weight.reshape(rows // LANES, LANES)
    weight_line = det_weight.reshape(1, rows)
    prior = star_prior.reshape(star_prior.shape[0] // LANES, LANES)

    def exchange(x):
        y = lax.all_to_all(x.reshape(peers, -1, LANES), everyone, split_axis=0, concat_axis=0, tiled=True)
        return y.reshape(x.shape)

    def over_pix(x):
        return lax.all_to_all(x, "pix", split_axis=0, concat_axis=0, tiled=True)

    pixes = lax.axis_size("pix")
    me = lax.axis_index("pix").reshape(1)

    def norm_exchange(send, keep):
        got = lax.ppermute(send, "pix", [(i, i ^ 1) for i in range(pixes)])
        parts = []
        for d in range(pixes // 2):
            part = keep[d] + got[d]
            if d > 0:
                part = lax.ppermute(part, "pix", [(i, (i + 2 * d) % pixes) for i in range(pixes)])
            parts.append(part)
        return parts

    order, row, lane, start, count, line = route(owner)
    pred, pay = place_first(coef_init, design, row, lane, start, count, slot, weight_rows, outlier_mask, cap)
    pay = exchange(pay)
    send = gram(me, design, weight_line, outlier_mask, 0, exps, False)
    keep = gram(me, design, weight_line, outlier_mask, 0, exps, True)
    gram_0 = norm_exchange(send, keep)
    ret, kept = owner_first(pay, star_ref, prior, cap)
    ret = exchange(ret)
    inverse_0 = invert_first(gram_0, terms, SPLIT)
    inverse_0 = invert_rest(inverse_0, SPLIT)
    right = right_sides(0, ret, order, start, count, line, pred, design, weight_line, outlier_mask, exps)
    right = over_pix(right)
    send = gram(me, design, weight_line, outlier_mask, 1, exps, False)
    keep = gram(me, design, weight_line, outlier_mask, 1, exps, True)
    gram_1 = norm_exchange(send, keep)
    upd = solve(right, inverse_0)
    upd = over_pix(upd)
    pred, pay, coef = place_next(coef_init, upd, design, row, lane, start, count, cap)
    pay = exchange(pay)
    ret, means = owner_next(pay, kept, star_ref, prior, cap)
    ret = exchange(ret)
    inverse_1 = invert(gram_1, terms)
    right = right_sides(1, ret, order, start, count, line, pred, design, weight_line, outlier_mask, exps)
    right = over_pix(right)
    coef = solve_last(me, coef, right, inverse_1)
    coef = over_pix(coef)
    return (coef, means)


def solution(mesh):
    placed = (
        P(None, ("pix", "exp")),
        P(("pix", "exp")),
        P(None, ("pix", "exp")),
        P(("pix", "exp"), None),
        P(("pix", "exp")),
        P("exp", None, None),
        P(None, ("pix", "exp")),
        P(("pix", "exp")),
    )
    return jax.shard_map(
        on_device,
        mesh=mesh,
        in_specs=placed,
        out_specs=(P("exp", None, None), P(None, ("pix", "exp"))),
        check_vma=False,
    )
```

```python
import functools

import jax
import jax.numpy as jnp
from jax import lax
from jax.experimental import pallas as pl
from jax.experimental.pallas import tpu as pltpu
from jax.sharding import PartitionSpec as P


RIDGE = 0.5
LANES = 128
F32 = jnp.float32
BF16 = jnp.bfloat16
GRANT = 16 << 20
FLOPS_PER_US = 10**9
SPLIT = 10
NT = (((1,), (1,)), ((), ()))
TN = (((0,), (0,)), ((), ()))


def iota(shape, axis):
    return lax.broadcasted_iota(jnp.int32, shape, axis)


def lane_gather(row, index):
    table = jnp.broadcast_to(row, index.shape)
    return jnp.take_along_axis(table, index, axis=1, mode="promise_in_bounds")


def call(body, out_shape, scratch=(), micros=1, size=0, in_specs=None):
    specs = {} if in_specs is None else {"in_specs": in_specs}
    return pl.pallas_call(
        body,
        **specs,
        out_shape=out_shape,
        scratch_shapes=list(scratch),
        compiler_params=pltpu.CompilerParams(vmem_limit_bytes=GRANT),
        cost_estimate=pl.CostEstimate(flops=micros * FLOPS_PER_US, bytes_accessed=size, transcendentals=0),
    )


def route_body(owner_ref, order_ref, row_ref, lane_ref, start_ref, count_ref, line_ref, hot_ref, left_ref, right_ref):
    chunks = owner_ref.shape[0]
    sub = iota((LANES, LANES), 0)
    lane = iota((LANES, LANES), 1)
    wide_sub, wide_lane = iota((LANES, 2 * LANES), 0), iota((LANES, 2 * LANES), 1)
    prefix = jnp.where((wide_sub < wide_lane) | (wide_lane >= LANES), 1.0, 0.0).astype(BF16)

    def rank(r, base):
        at = pl.ds(pl.multiple_of(r * LANES, LANES), LANES)
        hot = jnp.where(owner_ref[pl.ds(r, 1), :] == sub, 1.0, 0.0)
        narrow = hot.astype(BF16)
        hot_ref[:, at] = narrow
        counts = jnp.dot(narrow, prefix, preferred_element_type=F32)
        order_ref[pl.ds(r, 1), :] = jnp.sum(hot * (counts[:, :LANES] + base), axis=0, keepdims=True).astype(jnp.int32)
        return base + counts[:, LANES:]

    counts = lax.fori_loop(0, chunks, rank, jnp.zeros((LANES, LANES), F32), unroll=8)
    high = jnp.floor(counts * (1.0 / LANES))
    split = jnp.concatenate([high, counts - high * LANES], axis=1).astype(BF16)
    below = jnp.where(lane < sub, 1.0, 0.0).astype(BF16)
    starts = jnp.dot(below, split, preferred_element_type=F32)
    start_ref[...] = (starts[:, :LANES] * LANES + starts[:, LANES:]).astype(jnp.int32)
    count_ref[...] = counts.astype(jnp.int32)
    line = jnp.sum(jnp.where(sub < lane, counts, 0.0), axis=0, keepdims=True)
    line8 = jnp.broadcast_to(line, (8, LANES))
    line_ref[...] = line8.astype(jnp.int32)
    high8 = jnp.floor(line8 * (1.0 / LANES))
    first = jnp.where(iota((8, LANES), 0) == 0, high8, line8 - high8 * LANES).astype(BF16)
    begin = jnp.dot(first, hot_ref[...], preferred_element_type=F32)
    sub_rows, lane_line = iota((chunks, LANES), 0), iota((1, LANES), 1).astype(F32)
    for r in range(chunks):
        at = slice(r * LANES, (r + 1) * LANES)
        place = order_ref[r : r + 1, :] + (begin[0:1, at] * LANES + begin[1:2, at]).astype(jnp.int32)
        order_ref[r : r + 1, :] = place
        hit = jnp.where((place >> 7) == sub_rows, 1.0, 0.0)
        left_ref[:chunks, at] = (hit * float(r)).astype(BF16)
        left_ref[chunks:, at] = (hit * lane_line).astype(BF16)
        right_ref[:, at] = jnp.where((place & 127) == sub, 1.0, 0.0).astype(BF16)
    held = lax.dot_general(left_ref[...], right_ref[...], NT, preferred_element_type=F32)
    row_ref[...] = held[:chunks].astype(jnp.int32)
    lane_ref[...] = held[chunks:].astype(jnp.int32)


def route(owner):
    chunks = owner.shape[0]
    rows = chunks * LANES
    line = jax.ShapeDtypeStruct(owner.shape, jnp.int32)
    plane = jax.ShapeDtypeStruct((LANES, LANES), jnp.int32)
    return call(
        route_body,
        (line, line, line, plane, plane, jax.ShapeDtypeStruct((8, LANES), jnp.int32)),
        (pltpu.VMEM((LANES, rows), BF16), pltpu.VMEM((2 * chunks, rows), BF16), pltpu.VMEM((LANES, rows), BF16)),
        micros=4,
        size=rows * 8,
    )(owner)


def pieces(x):
    a = x.astype(BF16).astype(F32)
    b = (x - a).astype(BF16).astype(F32)
    c = ((x - a) - b).astype(BF16).astype(F32)
    return (a, b, c)


def lookup_rows(table, base, chunks, row, lane, values):
    found = [jnp.zeros((8, LANES), F32)] * values
    for r in range(chunks):
        hit = row == r
        for v in range(values):
            at = base[v] + r
            found[v] = jnp.where(hit, lane_gather(table[at : at + 1, :], lane), found[v])
    return found


def place_body(cap, first, *refs):
    if first:
        (coef_ref, design_ref, row_ref, lane_ref, start_ref, count_ref, slot_ref, weight_ref, mask_ref) = refs[:9]
        pred_ref, pay_ref, vals, dense, spread = refs[9:]
        coef = coef_ref[...]
    else:
        coef_ref, upd_ref, design_ref, row_ref, lane_ref, start_ref, count_ref = refs[:7]
        pred_ref, pay_ref, new_ref, vals, dense, spread = refs[7:]
        coef = coef_ref[...] + upd_ref[...]
        new_ref[...] = coef
    exps = coef.shape[0]
    rows = design_ref.shape[1]
    chunks = rows // LANES
    width = rows // exps
    per = width // LANES
    maps = coef.astype(BF16)
    for e in range(exps):
        pred = jnp.dot(maps[e], design_ref[:, e * width : (e + 1) * width], preferred_element_type=F32)
        pred_ref[:, e * width : (e + 1) * width] = pred
        for c in range(2):
            for q in range(per):
                r = c * chunks + e * per + q
                vals[r : r + 1, :] = pred[c : c + 1, q * LANES : (q + 1) * LANES]
    if first:
        for r in range(chunks):
            at = slice(r * LANES, (r + 1) * LANES)
            code = slot_ref[r : r + 1, :] + (mask_ref[0:1, at] << 10) + (mask_ref[1:2, at] << 11)
            vals[2 * chunks + r : 2 * chunks + r + 1, :] = code.astype(F32)
        vals[3 * chunks : 4 * chunks, :] = weight_ref[...]
    values = 4 if first else 2
    width_out = 4 if first else 2
    lane8 = iota((8, LANES), 1)

    def gather(d, carry):
        at = pl.ds(pl.multiple_of(d * 8, 8), 8)
        found = lookup_rows(vals, [v * chunks for v in range(values)], chunks, row_ref[at, :], lane_ref[at, :], values)
        for v in range(values):
            for k, piece in enumerate(pieces(found[v])):
                dense[at, (3 * v + k) * LANES : (3 * v + k + 1) * LANES] = piece
        return carry

    lax.fori_loop(0, chunks // 8, gather, 0, unroll=2 if first else 3)
    row_of = start_ref[...] >> 7
    column = iota((LANES, chunks), 1)
    pick = jnp.concatenate(
        [jnp.where(row_of[:, :chunks] + k == column, 1.0, 0.0) for k in range(2)], axis=0
    ).astype(BF16)
    spread[...] = jnp.dot(pick, dense[...].astype(BF16), preferred_element_type=F32)

    def tile(d, carry):
        at = pl.ds(pl.multiple_of(d * 8, 8), 8)
        spot = (start_ref[at, :] & 127) + lane8
        index, near = spot & 127, spot < LANES
        held = lane8 < count_ref[at, :]
        found = []
        for v in range(values):
            rows_of = []
            for k in range(2):
                part = [
                    spread[pl.ds(pl.multiple_of(d * 8 + k * LANES, 8), 8), (3 * v + j) * LANES : (3 * v + j + 1) * LANES]
                    for j in range(3)
                ]
                whole = part[0] + (part[1] + part[2])
                rows_of.append(jnp.take_along_axis(whole, index, axis=1, mode="promise_in_bounds"))
            found.append(jnp.where(held, jnp.where(near, rows_of[0], rows_of[1]), 0.0))
        if first:
            spare = LANES - cap
            code, weight = found[2].astype(jnp.int32), found[3]
            found[2] = (code & 1023).astype(F32)
            found[3] = weight * ((code >> 10) & 1).astype(F32)
            later = weight * (code >> 11).astype(F32)
            for v in range(3):
                moved = pltpu.roll(later, (cap - v * spare) % LANES, 1)
                found[v] = jnp.where(lane8 < cap, found[v], moved)
        for v in range(width_out):
            pay_ref[pl.ds(d * 8 * width_out + v, 8, stride=width_out), :] = found[v]
        return carry

    lax.fori_loop(0, LANES // 8, tile, 0, unroll=4)


def place_scratch(values, chunks):
    return (
        pltpu.VMEM((values * chunks, LANES), F32),
        pltpu.VMEM((chunks, 3 * values * LANES), F32),
        pltpu.VMEM((2 * LANES, 3 * values * LANES), F32),
    )


def place_first(coef, design, row, lane, start, count, slot, weight, mask, cap):
    rows = design.shape[1]
    return call(
        functools.partial(place_body, cap, True),
        (pltpu.HBM((2, rows), F32), jax.ShapeDtypeStruct((4 * LANES, LANES), F32)),
        place_scratch(4, rows // LANES),
        micros=5,
        size=2 * design.size,
    )(coef, design, row, lane, start, count, slot, weight, mask)


def place_next(coef, upd, design, row, lane, start, count, cap):
    rows = design.shape[1]
    return call(
        functools.partial(place_body, cap, False),
        (
            pltpu.HBM((2, rows), F32),
            jax.ShapeDtypeStruct((2 * LANES, LANES), F32),
            jax.ShapeDtypeStruct(coef.shape, F32),
        ),
        place_scratch(2, rows // LANES),
        micros=3,
        size=2 * design.size,
    )(coef, upd, design, row, lane, start, count)


def owner_body(cap, first, *refs):
    if first:
        pay_ref, ref_ref, prior_ref, ret_ref, kept_ref, parts, id_ref = refs
        width = 4
    else:
        pay_ref, kept_ref, ref_ref, prior_ref, ret_ref, mean_ref, parts, id_ref = refs
        width = 2
    lane8 = iota((8, LANES), 1)
    sub8 = iota((8, LANES), 0)
    sub = iota((LANES, LANES), 0)
    spare = LANES - cap

    def split(g, carry):
        def plane(v):
            return pay_ref[pl.ds(g * 8 * width + v, 8, stride=width), :]

        at = pl.ds(pl.multiple_of(g * 8, 8), 8)
        if first:
            p0, p1, ids, weight = plane(0), plane(1), plane(2), plane(3)
            later = jnp.zeros((8, LANES), F32)
            for v, source in enumerate((p0, p1, ids)):
                moved = pltpu.roll(source, (v * spare - cap) % LANES, 1)
                later = jnp.where((lane8 >= v * spare) & (lane8 < (v + 1) * spare), moved, later)
            kept_ref[0, at, :] = ids
            kept_ref[1, at, :] = later
            weight = jnp.where(lane8 < cap, weight, 0.0)
            id_ref[at, :] = ids.astype(jnp.int32)
        else:
            p0, p1, weight = plane(0), plane(1), kept_ref[1, at, :]
            id_ref[at, :] = kept_ref[0, at, :].astype(jnp.int32)
        for v, x in enumerate((weight * p0, weight * p1, weight)):
            for k, piece in enumerate(pieces(x)):
                parts[3 * v + k, at, :] = piece
        return carry

    lax.fori_loop(0, LANES // 8, split, 0, unroll=4)
    group = 8

    def accumulate(g, total):
        left, right = [], []
        for s in range(group):
            src = g * group + s
            ids = id_ref[pl.ds(src, 1), :]
            hit = (ids >> 7) == sub8
            left.append(
                jnp.concatenate(
                    [jnp.where(hit, parts[k, pl.ds(src, 1), :], 0.0) for k in range(9)], axis=0
                ).astype(BF16)
            )
            right.append(jnp.where((ids & 127) == sub, 1.0, 0.0).astype(BF16))
        return total + lax.dot_general(
            jnp.concatenate(right, axis=1), jnp.concatenate(left, axis=1), NT, preferred_element_type=F32
        )

    total = lax.fori_loop(0, LANES // group, accumulate, jnp.zeros((LANES, 72), F32), unroll=4).T
    sums = [total[24 * v : 24 * v + 8] + total[24 * v + 8 : 24 * v + 16] + total[24 * v + 16 : 24 * v + 24] for v in range(3)]
    rows = prior_ref.shape[0]
    means = [[], []]
    for h in range(rows):
        prior = prior_ref[h : h + 1, :]
        for c in range(2):
            ref = ref_ref[c : c + 1, h * LANES : (h + 1) * LANES]
            mean = (prior * ref + sums[c][h : h + 1]) / (prior + sums[2][h : h + 1])
            means[c].append(mean)
            if not first:
                mean_ref[c : c + 1, h * LANES : (h + 1) * LANES] = mean

    def look(g, carry):
        at = pl.ds(pl.multiple_of(g * 8, 8), 8)
        ids = id_ref[at, :]
        low, high = ids & 127, ids >> 7
        for c in range(2):
            found = jnp.zeros((8, LANES), F32)
            for h in range(rows):
                found = jnp.where(high == h, lane_gather(means[c][h], low), found)
            ret_ref[pl.ds(g * 16 + c, 8, stride=2), :] = found
        return carry

    lax.fori_loop(0, LANES // 8, look, 0, unroll=4)


def owner_first(pay, star_ref, star_prior, cap):
    return call(
        functools.partial(owner_body, cap, True),
        (
            jax.ShapeDtypeStruct((2 * LANES, LANES), F32),
            pltpu.HBM((2, LANES, LANES), F32),
        ),
        (pltpu.VMEM((9, LANES, LANES), F32), pltpu.VMEM((LANES, LANES), jnp.int32)),
        micros=4,
        size=pay.size * 4,
    )(pay, star_ref, star_prior)


def owner_next(pay, kept, star_ref, star_prior, cap):
    return call(
        functools.partial(owner_body, cap, False),
        (jax.ShapeDtypeStruct((2 * LANES, LANES), F32), jax.ShapeDtypeStruct(star_ref.shape, F32)),
        (
            pltpu.VMEM((9, LANES, LANES), F32),
            pltpu.VMEM((LANES, LANES), jnp.int32),
        ),
        micros=3,
        size=pay.size * 4,
    )(pay, kept, star_ref, star_prior)


def right_body(step_index, *refs):
    ret_ref, order_ref, start_ref, count_ref, line_ref, pred_ref, design_ref, weight_ref, mask_ref = refs[:9]
    right_ref, shifted, dense, back = refs[9:]
    chunks = order_ref.shape[0]
    exps = right_ref.shape[0]
    rows = pred_ref.shape[1]
    width = rows // exps
    lane8 = iota((8, LANES), 1)

    def shift(d, carry):
        at = pl.ds(pl.multiple_of(d * 8, 8), 8)
        offset = start_ref[at, :] & 127
        end = offset + count_ref[at, :]
        index = (lane8 - offset) & 127
        near = (lane8 >= offset) & (lane8 < end)
        far = lane8 + LANES < end
        for c in range(2):
            moved = jnp.take_along_axis(ret_ref[pl.ds(d * 16 + c, 8, stride=2), :], index, axis=1, mode="promise_in_bounds")
            for k, keep in enumerate((near, far)):
                for j, piece in enumerate(pieces(jnp.where(keep, moved, 0.0))):
                    shifted[pl.ds(pl.multiple_of(d * 8 + k * LANES, 8), 8), (3 * c + j) * LANES : (3 * c + j + 1) * LANES] = piece
        return carry

    lax.fori_loop(0, LANES // 8, shift, 0, unroll=4)
    row_of = line_ref[0:1, :] >> 7
    sub_rows = iota((chunks, LANES), 0)
    pick = jnp.concatenate([jnp.where(row_of + k == sub_rows, 1.0, 0.0) for k in range(2)], axis=1).astype(BF16)
    spread = jnp.dot(pick, shifted[...].astype(BF16), preferred_element_type=F32)
    for c in range(2):
        part = [spread[:, (3 * c + j) * LANES : (3 * c + j + 1) * LANES] for j in range(3)]
        dense[c * chunks : (c + 1) * chunks, :] = part[0] + (part[1] + part[2])

    line_weight = weight_ref[...] * mask_ref[step_index : step_index + 1, :].astype(F32)
    for d in range(chunks // 8):
        order = order_ref[8 * d : 8 * d + 8, :]
        found = lookup_rows(dense, [0, chunks], chunks, order >> 7, order & 127, 2)
        for c in range(2):
            for s in range(8):
                r = 8 * d + s
                back[c : c + 1, r * LANES : (r + 1) * LANES] = found[c][s : s + 1]
    for e in range(exps):
        at = slice(e * width, (e + 1) * width)
        weighted = (design_ref[:, at].astype(F32) * line_weight[:, at]).astype(BF16)
        residual = (back[:, at] - pred_ref[:, at]).astype(BF16)
        right_ref[e] = lax.dot_general(residual, weighted, NT, preferred_element_type=F32)


def right_sides(k, ret, order, start, count, line, pred, design, weight, mask, exps):
    terms, rows = design.shape
    chunks = rows // LANES
    return call(
        functools.partial(right_body, k),
        jax.ShapeDtypeStruct((exps, 2, terms), F32),
        (
            pltpu.VMEM((2 * LANES, 6 * LANES), F32),
            pltpu.VMEM((2 * chunks, LANES), F32),
            pltpu.VMEM((2, rows), F32),
        ),
        micros=2,
        size=2 * design.size,
    )(ret, order, start, count, line, pred, design, weight, mask)


def exposure_gram(k, design_ref, weight_ref, mask_ref):
    design = design_ref[...]
    weight = weight_ref[...] * mask_ref[k : k + 1, :].astype(F32)
    weighted = (design.astype(F32) * weight).astype(BF16)
    return 0.5 * lax.dot_general(
        jnp.concatenate([weighted, design], axis=1),
        jnp.concatenate([design, weighted], axis=1),
        NT,
        preferred_element_type=F32,
    )


def pack(gram, out_ref):
    terms = gram.shape[0]
    rest = terms - LANES
    out_ref[0, :terms, :] = gram[:, :LANES]
    out_ref[0, terms:, :] = jnp.zeros((rest, LANES), F32)
    out_ref[0, terms:, :rest] = gram[LANES:, LANES:]


def gram_body(k, me_ref, design_ref, weight_ref, mask_ref, gram_ref):
    pack(exposure_gram(k, design_ref, weight_ref, mask_ref), gram_ref)


def gram(me, design, weight, mask, k, exps, mine):
    terms, rows = design.shape
    width = rows // exps
    packed = 2 * terms - LANES
    half = exps // 2

    def exposure(d, me_ref):
        return 2 * lax.rem(lax.div(me_ref[0], 2) + d, half) + lax.rem(me_ref[0] + (0 if mine else 1), 2)

    return pl.pallas_call(
        functools.partial(gram_body, k),
        grid_spec=pltpu.PrefetchScalarGridSpec(
            num_scalar_prefetch=1,
            grid=(half,),
            in_specs=[
                pl.BlockSpec((terms, width), lambda d, me_ref: (0, exposure(d, me_ref))),
                pl.BlockSpec((1, width), lambda d, me_ref: (0, exposure(d, me_ref))),
                pl.BlockSpec((2, width), lambda d, me_ref: (0, exposure(d, me_ref))),
            ],
            out_specs=pl.BlockSpec((1, packed, LANES), lambda d, me_ref: (d, 0, 0)),
        ),
        out_shape=jax.ShapeDtypeStruct((half, packed, LANES), F32),
        compiler_params=pltpu.CompilerParams(vmem_limit_bytes=GRANT),
        cost_estimate=pl.CostEstimate(
            flops=2 * FLOPS_PER_US, bytes_accessed=2 * design.size, transcendentals=0
        ),
    )(me, design, weight, mask)


def eliminate(panel, base, tile):
    sub = iota((8, LANES), 0)
    lane = iota((8, LANES), 1)
    panel = list(panel)
    index = jnp.zeros((8, LANES), jnp.int32) + base
    cols = [jnp.take_along_axis(panel[tile], index + j, axis=1, mode="promise_in_bounds") for j in range(8)]
    for j in range(8):
        inverse = 1.0 / jnp.broadcast_to(cols[j][j : j + 1], (8, LANES))
        mine = sub == j
        panel[tile] = jnp.where(lane == base + j, jnp.where(mine, 1.0, 0.0), panel[tile])

        def sweep(x):
            row = jnp.broadcast_to(x[j : j + 1], (8, LANES)) * inverse
            return jnp.where(mine, row, x - cols[j] * row)

        for m in range(j + 1, 8):
            cols[m] = sweep(cols[m])
        panel = [sweep(x) for x in panel]
    inside = (lane >= base) & (lane < base + 8)
    panel[tile] = jnp.where(inside, -panel[tile], panel[tile])
    return panel


def outside(k, rows):
    lane = iota((rows, 2 * LANES), 1)
    return jnp.where((lane >= k * 8) & (lane < k * 8 + 8), 0.0, 1.0)


def block_rows(k):
    return pl.ds(pl.multiple_of(k * 8, 8), 8)


def update_all(mat, k, before, swept):
    r, q = pieces(jnp.concatenate(before, axis=1)), pieces(jnp.concatenate(swept, axis=1))
    left = jnp.concatenate([r[0], r[0], r[0], r[1], r[1], r[2]], axis=0).astype(BF16)
    right = jnp.concatenate([q[0], q[1], q[2], q[0], q[1], q[0]], axis=0).astype(BF16)
    change = lax.dot_general(left, right, TN, preferred_element_type=F32)
    mat[...] = mat[...] * outside(k, 1) - change[: mat.shape[0]]
    mat[block_rows(k), :] = jnp.concatenate(swept, axis=1)


def update_next(mat, k, swept, base, tile):
    at = block_rows(jnp.minimum(k + 1, mat.shape[0] // 8 - 1))
    rows = [mat[at, t * LANES : (t + 1) * LANES] for t in range(2)]
    keep = outside(k, 8)
    index = jnp.zeros((8, LANES), jnp.int32) + base
    fresh = [rows[t] * keep[:, t * LANES : (t + 1) * LANES] for t in range(2)]
    for j in range(8):
        col = jnp.take_along_axis(rows[tile], index + j, axis=1, mode="promise_in_bounds")
        fresh = [fresh[t] - col * jnp.broadcast_to(swept[t][j : j + 1], (8, LANES)) for t in range(2)]
    return fresh


def sweep_range(mat, low, high):
    start = low // 16
    base = low * 8 - start * LANES
    first = [mat[low * 8 : low * 8 + 8, t * LANES : (t + 1) * LANES] for t in range(2)]
    swept = eliminate(first, base, start)
    carry = (tuple(first), tuple(swept), tuple(update_next(mat, low, swept, base, start)))
    for tile in range(2):
        begin, end = max(low + 1, 16 * tile), min(high, 16 * (tile + 1))

        def step(k, carry):
            before, swept, panel = carry
            base = k * 8 - tile * LANES
            fresh = eliminate(panel, base, tile)
            update_all(mat, k - 1, before, swept)
            return (panel, tuple(fresh), tuple(update_next(mat, k, fresh, base, tile)))

        if begin < end:
            carry = lax.fori_loop(begin, end, step, carry)
    update_all(mat, high - 1, carry[0], carry[1])


def unpack(gram_refs, mat):
    terms = mat.shape[0]
    rest = terms - LANES
    total = functools.reduce(lambda a, b: a + b, [ref[...] for ref in gram_refs])
    square = jnp.concatenate([total[LANES:terms], jnp.zeros((LANES - rest, LANES), F32)], axis=0)
    mat[:, :LANES] = total[:terms]
    mat[:LANES, LANES:] = square.T
    mat[LANES:, LANES:] = total[terms:]
    mat[...] = mat[...] + jnp.where(iota((terms, 2 * LANES), 0) == iota((terms, 2 * LANES), 1), RIDGE, 0.0)


def invert_body(*refs):
    *gram_refs, out_ref, mat = refs
    unpack(gram_refs, mat)
    sweep_range(mat, 0, mat.shape[0] // 8)
    out_ref[...] = -mat[...]


def invert(grams, terms):
    return call(
        invert_body,
        pltpu.HBM((terms, 2 * LANES), F32),
        (pltpu.VMEM((terms, 2 * LANES), F32),),
        micros=8,
        size=4 * len(grams) * grams[0].size,
    )(*grams)


def invert_first_body(high, *refs):
    *gram_refs, mat = refs
    unpack(gram_refs, mat)
    sweep_range(mat, 0, high)


def invert_rest_body(low, part_ref, out_ref):
    out_ref[...] = part_ref[...]
    sweep_range(out_ref, low, out_ref.shape[0] // 8)
    out_ref[...] = -out_ref[...]


def invert_first(grams, terms, high):
    return call(
        functools.partial(invert_first_body, high),
        jax.ShapeDtypeStruct((terms, 2 * LANES), F32),
        micros=4,
        size=4 * len(grams) * grams[0].size,
    )(*grams)


def invert_rest(part, low):
    return call(
        functools.partial(invert_rest_body, low),
        jax.ShapeDtypeStruct(part.shape, F32),
        micros=4,
        size=8 * part.size,
    )(part)


def solve_body(last, *refs):
    if last:
        me_ref, coef_ref, right_ref, inverse_ref, out_ref = refs
    else:
        right_ref, inverse_ref, out_ref = refs
    terms = inverse_ref.shape[0]
    right = right_ref[0]
    for s in range(1, right_ref.shape[0]):
        right = right + right_ref[s]
    update = jnp.dot(right, inverse_ref[...], precision=lax.Precision.HIGHEST, preferred_element_type=F32)[:, :terms]
    if last:
        update = coef_ref[me_ref[0]] + update
    for s in range(right_ref.shape[0]):
        out_ref[s] = update


def solve(right, inverse):
    shape = jax.ShapeDtypeStruct(right.shape, F32)
    return call(functools.partial(solve_body, False), shape, micros=1, size=inverse.size * 4)(right, inverse)


def solve_last(me, coef, right, inverse):
    shape = jax.ShapeDtypeStruct(right.shape, F32)
    specs = [pl.BlockSpec(memory_space=pltpu.SMEM)] + [pl.BlockSpec()] * 3
    return call(functools.partial(solve_body, True), shape, micros=1, size=inverse.size * 4, in_specs=specs)(
        me, coef, right, inverse
    )


def on_device(design, det_weight, outlier_mask, star_owner, star_slot, coef_init, star_ref, star_prior):
    everyone = ("pix", "exp")
    peers = lax.axis_size(everyone)
    terms, rows = design.shape
    exps = coef_init.shape[0]
    cap = 2 * rows // peers
    owner = star_owner.reshape(rows // LANES, LANES)
    slot = star_slot.reshape(rows // LANES, LANES)
    weight_rows = det_weight.reshape(rows // LANES, LANES)
    weight_line = det_weight.reshape(1, rows)
    prior = star_prior.reshape(star_prior.shape[0] // LANES, LANES)

    def exchange(x):
        y = lax.all_to_all(x.reshape(peers, -1, LANES), everyone, split_axis=0, concat_axis=0, tiled=True)
        return y.reshape(x.shape)

    def over_pix(x):
        return lax.all_to_all(x, "pix", split_axis=0, concat_axis=0, tiled=True)

    pixes = lax.axis_size("pix")
    me = lax.axis_index("pix").reshape(1)

    def norm_exchange(send, keep):
        got = lax.ppermute(send, "pix", [(i, i ^ 1) for i in range(pixes)])
        parts = []
        for d in range(pixes // 2):
            part = keep[d] + got[d]
            if d > 0:
                part = lax.ppermute(part, "pix", [(i, (i + 2 * d) % pixes) for i in range(pixes)])
            parts.append(part)
        return parts

    order, row, lane, start, count, line = route(owner)
    pred, pay = place_first(coef_init, design, row, lane, start, count, slot, weight_rows, outlier_mask, cap)
    pay = exchange(pay)
    send = gram(me, design, weight_line, outlier_mask, 0, exps, False)
    keep = gram(me, design, weight_line, outlier_mask, 0, exps, True)
    gram_0 = norm_exchange(send, keep)
    ret, kept = owner_first(pay, star_ref, prior, cap)
    ret = exchange(ret)
    inverse_0 = invert_first(gram_0, terms, SPLIT)
    inverse_0 = invert_rest(inverse_0, SPLIT)
    right = right_sides(0, ret, order, start, count, line, pred, design, weight_line, outlier_mask, exps)
    right = over_pix(right)
    send = gram(me, design, weight_line, outlier_mask, 1, exps, False)
    keep = gram(me, design, weight_line, outlier_mask, 1, exps, True)
    gram_1 = norm_exchange(send, keep)
    upd = solve(right, inverse_0)
    upd = over_pix(upd)
    pred, pay, coef = place_next(coef_init, upd, design, row, lane, start, count, cap)
    pay = exchange(pay)
    ret, means = owner_next(pay, kept, star_ref, prior, cap)
    ret = exchange(ret)
    inverse_1 = invert(gram_1, terms)
    right = right_sides(1, ret, order, start, count, line, pred, design, weight_line, outlier_mask, exps)
    right = over_pix(right)
    coef = solve_last(me, coef, right, inverse_1)
    coef = over_pix(coef)
    return (coef, means)


def solution(mesh):
    placed = (
        P(None, ("pix", "exp")),
        P(("pix", "exp")),
        P(None, ("pix", "exp")),
        P(("pix", "exp"), None),
        P(("pix", "exp")),
        P("exp", None, None),
        P(None, ("pix", "exp")),
        P(("pix", "exp")),
    )
    return jax.shard_map(
        on_device,
        mesh=mesh,
        in_specs=placed,
        out_specs=(P("exp", None, None), P(None, ("pix", "exp"))),
        check_vma=False,
    )
```

```python
import functools

import jax
import jax.numpy as jnp
from jax import lax
from jax.experimental import pallas as pl
from jax.experimental.pallas import tpu as pltpu
from jax.sharding import PartitionSpec as P


RIDGE = 0.5
LANES = 128
F32 = jnp.float32
BF16 = jnp.bfloat16
GRANT = 16 << 20
FLOPS_PER_US = 10**9
SPLIT = 10
NT = (((1,), (1,)), ((), ()))
TN = (((0,), (0,)), ((), ()))


def iota(shape, axis):
    return lax.broadcasted_iota(jnp.int32, shape, axis)


def lane_gather(row, index):
    table = jnp.broadcast_to(row, index.shape)
    return jnp.take_along_axis(table, index, axis=1, mode="promise_in_bounds")


def call(body, out_shape, scratch=(), micros=1, size=0, in_specs=None):
    specs = {} if in_specs is None else {"in_specs": in_specs}
    return pl.pallas_call(
        body,
        **specs,
        out_shape=out_shape,
        scratch_shapes=list(scratch),
        compiler_params=pltpu.CompilerParams(vmem_limit_bytes=GRANT),
        cost_estimate=pl.CostEstimate(flops=micros * FLOPS_PER_US, bytes_accessed=size, transcendentals=0),
    )


def route_body(owner_ref, order_ref, row_ref, lane_ref, start_ref, count_ref, line_ref, hot_ref, left_ref, right_ref):
    chunks = owner_ref.shape[0]
    sub = iota((LANES, LANES), 0)
    lane = iota((LANES, LANES), 1)
    wide_sub, wide_lane = iota((LANES, 2 * LANES), 0), iota((LANES, 2 * LANES), 1)
    prefix = jnp.where((wide_sub < wide_lane) | (wide_lane >= LANES), 1.0, 0.0).astype(BF16)

    def rank(r, base):
        at = pl.ds(pl.multiple_of(r * LANES, LANES), LANES)
        hot = jnp.where(owner_ref[pl.ds(r, 1), :] == sub, 1.0, 0.0)
        narrow = hot.astype(BF16)
        hot_ref[:, at] = narrow
        counts = jnp.dot(narrow, prefix, preferred_element_type=F32)
        order_ref[pl.ds(r, 1), :] = jnp.sum(hot * (counts[:, :LANES] + base), axis=0, keepdims=True).astype(jnp.int32)
        return base + counts[:, LANES:]

    counts = lax.fori_loop(0, chunks, rank, jnp.zeros((LANES, LANES), F32), unroll=24)
    high = jnp.floor(counts * (1.0 / LANES))
    split = jnp.concatenate([high, counts - high * LANES], axis=1).astype(BF16)
    below = jnp.where(lane < sub, 1.0, 0.0).astype(BF16)
    starts = jnp.dot(below, split, preferred_element_type=F32)
    start_ref[...] = (starts[:, :LANES] * LANES + starts[:, LANES:]).astype(jnp.int32)
    count_ref[...] = counts.astype(jnp.int32)
    line = jnp.sum(jnp.where(sub < lane, counts, 0.0), axis=0, keepdims=True)
    line8 = jnp.broadcast_to(line, (8, LANES))
    line_ref[...] = line8.astype(jnp.int32)
    high8 = jnp.floor(line8 * (1.0 / LANES))
    first = jnp.where(iota((8, LANES), 0) == 0, high8, line8 - high8 * LANES).astype(BF16)
    begin = jnp.dot(first, hot_ref[...], preferred_element_type=F32)
    sub_rows, lane_line = iota((chunks, LANES), 0), iota((1, LANES), 1).astype(F32)
    for r in range(chunks):
        at = slice(r * LANES, (r + 1) * LANES)
        place = order_ref[r : r + 1, :] + (begin[0:1, at] * LANES + begin[1:2, at]).astype(jnp.int32)
        order_ref[r : r + 1, :] = place
        hit = jnp.where((place >> 7) == sub_rows, 1.0, 0.0)
        left_ref[:chunks, at] = (hit * float(r)).astype(BF16)
        left_ref[chunks:, at] = (hit * lane_line).astype(BF16)
        right_ref[:, at] = jnp.where((place & 127) == sub, 1.0, 0.0).astype(BF16)
    held = lax.dot_general(left_ref[...], right_ref[...], NT, preferred_element_type=F32)
    row_ref[...] = held[:chunks].astype(jnp.int32)
    lane_ref[...] = held[chunks:].astype(jnp.int32)


def route(owner):
    chunks = owner.shape[0]
    rows = chunks * LANES
    line = jax.ShapeDtypeStruct(owner.shape, jnp.int32)
    plane = jax.ShapeDtypeStruct((LANES, LANES), jnp.int32)
    return call(
        route_body,
        (line, line, line, plane, plane, jax.ShapeDtypeStruct((8, LANES), jnp.int32)),
        (pltpu.VMEM((LANES, rows), BF16), pltpu.VMEM((2 * chunks, rows), BF16), pltpu.VMEM((LANES, rows), BF16)),
        micros=4,
        size=rows * 8,
    )(owner)


def pieces(x):
    a = x.astype(BF16).astype(F32)
    b = (x - a).astype(BF16).astype(F32)
    c = ((x - a) - b).astype(BF16).astype(F32)
    return (a, b, c)


def lookup_rows(table, base, chunks, row, lane, values):
    found = [jnp.zeros((8, LANES), F32)] * values
    for r in range(chunks):
        hit = row == r
        for v in range(values):
            at = base[v] + r
            found[v] = jnp.where(hit, lane_gather(table[at : at + 1, :], lane), found[v])
    return found


def place_body(cap, first, *refs):
    if first:
        (coef_ref, design_ref, row_ref, lane_ref, start_ref, count_ref, slot_ref, weight_ref, mask_ref) = refs[:9]
        pred_ref, pay_ref, vals, dense, spread = refs[9:]
        coef = coef_ref[...]
    else:
        coef_ref, upd_ref, design_ref, row_ref, lane_ref, start_ref, count_ref = refs[:7]
        pred_ref, pay_ref, new_ref, vals, dense, spread = refs[7:]
        coef = coef_ref[...] + upd_ref[...]
        new_ref[...] = coef
    exps = coef.shape[0]
    rows = design_ref.shape[1]
    chunks = rows // LANES
    width = rows // exps
    per = width // LANES
    maps = coef.astype(BF16)
    for e in range(exps):
        pred = jnp.dot(maps[e], design_ref[:, e * width : (e + 1) * width], preferred_element_type=F32)
        pred_ref[:, e * width : (e + 1) * width] = pred
        for c in range(2):
            for q in range(per):
                r = c * chunks + e * per + q
                vals[r : r + 1, :] = pred[c : c + 1, q * LANES : (q + 1) * LANES]
    if first:
        for r in range(chunks):
            at = slice(r * LANES, (r + 1) * LANES)
            code = slot_ref[r : r + 1, :] + (mask_ref[0:1, at] << 10) + (mask_ref[1:2, at] << 11)
            vals[2 * chunks + r : 2 * chunks + r + 1, :] = code.astype(F32)
        vals[3 * chunks : 4 * chunks, :] = weight_ref[...]
    values = 4 if first else 2
    width_out = 4 if first else 2
    lane8 = iota((8, LANES), 1)

    def gather(d, carry):
        at = pl.ds(pl.multiple_of(d * 8, 8), 8)
        found = lookup_rows(vals, [v * chunks for v in range(values)], chunks, row_ref[at, :], lane_ref[at, :], values)
        for v in range(values):
            for k, piece in enumerate(pieces(found[v])):
                dense[at, (3 * v + k) * LANES : (3 * v + k + 1) * LANES] = piece
        return carry

    lax.fori_loop(0, chunks // 8, gather, 0, unroll=6)
    row_of = start_ref[...] >> 7
    column = iota((LANES, chunks), 1)
    pick = jnp.concatenate(
        [jnp.where(row_of[:, :chunks] + k == column, 1.0, 0.0) for k in range(2)], axis=0
    ).astype(BF16)
    spread[...] = jnp.dot(pick, dense[...].astype(BF16), preferred_element_type=F32)

    def tile(d, carry):
        at = pl.ds(pl.multiple_of(d * 8, 8), 8)
        spot = (start_ref[at, :] & 127) + lane8
        index, near = spot & 127, spot < LANES
        held = lane8 < count_ref[at, :]
        found = []
        for v in range(values):
            rows_of = []
            for k in range(2):
                part = [
                    spread[pl.ds(pl.multiple_of(d * 8 + k * LANES, 8), 8), (3 * v + j) * LANES : (3 * v + j + 1) * LANES]
                    for j in range(3)
                ]
                whole = part[0] + (part[1] + part[2])
                rows_of.append(jnp.take_along_axis(whole, index, axis=1, mode="promise_in_bounds"))
            found.append(jnp.where(held, jnp.where(near, rows_of[0], rows_of[1]), 0.0))
        if first:
            spare = LANES - cap
            code, weight = found[2].astype(jnp.int32), found[3]
            found[2] = (code & 1023).astype(F32)
            found[3] = weight * ((code >> 10) & 1).astype(F32)
            later = weight * (code >> 11).astype(F32)
            for v in range(3):
                moved = pltpu.roll(later, (cap - v * spare) % LANES, 1)
                found[v] = jnp.where(lane8 < cap, found[v], moved)
        for v in range(width_out):
            pay_ref[pl.ds(d * 8 * width_out + v, 8, stride=width_out), :] = found[v]
        return carry

    lax.fori_loop(0, LANES // 8, tile, 0, unroll=8 if first else 16)


def place_scratch(values, chunks):
    return (
        pltpu.VMEM((values * chunks, LANES), F32),
        pltpu.VMEM((chunks, 3 * values * LANES), F32),
        pltpu.VMEM((2 * LANES, 3 * values * LANES), F32),
    )


def place_first(coef, design, row, lane, start, count, slot, weight, mask, cap):
    rows = design.shape[1]
    return call(
        functools.partial(place_body, cap, True),
        (pltpu.HBM((2, rows), F32), jax.ShapeDtypeStruct((4 * LANES, LANES), F32)),
        place_scratch(4, rows // LANES),
        micros=5,
        size=2 * design.size,
    )(coef, design, row, lane, start, count, slot, weight, mask)


def place_next(coef, upd, design, row, lane, start, count, cap):
    rows = design.shape[1]
    return call(
        functools.partial(place_body, cap, False),
        (
            pltpu.HBM((2, rows), F32),
            jax.ShapeDtypeStruct((2 * LANES, LANES), F32),
            jax.ShapeDtypeStruct(coef.shape, F32),
        ),
        place_scratch(2, rows // LANES),
        micros=3,
        size=2 * design.size,
    )(coef, upd, design, row, lane, start, count)


def owner_body(cap, first, *refs):
    if first:
        pay_ref, ref_ref, prior_ref, ret_ref, kept_ref, parts, id_ref = refs
        width = 4
    else:
        pay_ref, kept_ref, ref_ref, prior_ref, ret_ref, mean_ref, parts, id_ref = refs
        width = 2
    lane8 = iota((8, LANES), 1)
    sub8 = iota((8, LANES), 0)
    sub = iota((LANES, LANES), 0)
    spare = LANES - cap

    def split(g, carry):
        def plane(v):
            return pay_ref[pl.ds(g * 8 * width + v, 8, stride=width), :]

        at = pl.ds(pl.multiple_of(g * 8, 8), 8)
        if first:
            p0, p1, ids, weight = plane(0), plane(1), plane(2), plane(3)
            later = jnp.zeros((8, LANES), F32)
            for v, source in enumerate((p0, p1, ids)):
                moved = pltpu.roll(source, (v * spare - cap) % LANES, 1)
                later = jnp.where((lane8 >= v * spare) & (lane8 < (v + 1) * spare), moved, later)
            kept_ref[0, at, :] = ids
            kept_ref[1, at, :] = later
            weight = jnp.where(lane8 < cap, weight, 0.0)
            id_ref[at, :] = ids.astype(jnp.int32)
        else:
            p0, p1, weight = plane(0), plane(1), kept_ref[1, at, :]
            id_ref[at, :] = kept_ref[0, at, :].astype(jnp.int32)
        for v, x in enumerate((weight * p0, weight * p1, weight)):
            for k, piece in enumerate(pieces(x)):
                parts[3 * v + k, at, :] = piece
        return carry

    lax.fori_loop(0, LANES // 8, split, 0, unroll=16)
    group = 8

    def accumulate(g, total):
        left, right = [], []
        for s in range(group):
            src = g * group + s
            ids = id_ref[pl.ds(src, 1), :]
            hit = (ids >> 7) == sub8
            left.append(
                jnp.concatenate(
                    [jnp.where(hit, parts[k, pl.ds(src, 1), :], 0.0) for k in range(9)], axis=0
                ).astype(BF16)
            )
            right.append(jnp.where((ids & 127) == sub, 1.0, 0.0).astype(BF16))
        return total + lax.dot_general(
            jnp.concatenate(right, axis=1), jnp.concatenate(left, axis=1), NT, preferred_element_type=F32
        )

    total = lax.fori_loop(0, LANES // group, accumulate, jnp.zeros((LANES, 72), F32), unroll=16).T
    sums = [total[24 * v : 24 * v + 8] + total[24 * v + 8 : 24 * v + 16] + total[24 * v + 16 : 24 * v + 24] for v in range(3)]
    rows = prior_ref.shape[0]
    means = [[], []]
    for h in range(rows):
        prior = prior_ref[h : h + 1, :]
        for c in range(2):
            ref = ref_ref[c : c + 1, h * LANES : (h + 1) * LANES]
            mean = (prior * ref + sums[c][h : h + 1]) / (prior + sums[2][h : h + 1])
            means[c].append(mean)
            if not first:
                mean_ref[c : c + 1, h * LANES : (h + 1) * LANES] = mean

    def look(g, carry):
        at = pl.ds(pl.multiple_of(g * 8, 8), 8)
        ids = id_ref[at, :]
        low, high = ids & 127, ids >> 7
        for c in range(2):
            found = jnp.zeros((8, LANES), F32)
            for h in range(rows):
                found = jnp.where(high == h, lane_gather(means[c][h], low), found)
            ret_ref[pl.ds(g * 16 + c, 8, stride=2), :] = found
        return carry

    lax.fori_loop(0, LANES // 8, look, 0, unroll=16)


def owner_first(pay, star_ref, star_prior, cap):
    return call(
        functools.partial(owner_body, cap, True),
        (
            jax.ShapeDtypeStruct((2 * LANES, LANES), F32),
            pltpu.HBM((2, LANES, LANES), F32),
        ),
        (pltpu.VMEM((9, LANES, LANES), F32), pltpu.VMEM((LANES, LANES), jnp.int32)),
        micros=4,
        size=pay.size * 4,
    )(pay, star_ref, star_prior)


def owner_next(pay, kept, star_ref, star_prior, cap):
    return call(
        functools.partial(owner_body, cap, False),
        (jax.ShapeDtypeStruct((2 * LANES, LANES), F32), jax.ShapeDtypeStruct(star_ref.shape, F32)),
        (
            pltpu.VMEM((9, LANES, LANES), F32),
            pltpu.VMEM((LANES, LANES), jnp.int32),
        ),
        micros=3,
        size=pay.size * 4,
    )(pay, kept, star_ref, star_prior)


def right_body(step_index, *refs):
    ret_ref, order_ref, start_ref, count_ref, line_ref, pred_ref, design_ref, weight_ref, mask_ref = refs[:9]
    right_ref, shifted, dense, back = refs[9:]
    chunks = order_ref.shape[0]
    exps = right_ref.shape[0]
    rows = pred_ref.shape[1]
    width = rows // exps
    lane8 = iota((8, LANES), 1)

    def shift(d, carry):
        at = pl.ds(pl.multiple_of(d * 8, 8), 8)
        offset = start_ref[at, :] & 127
        end = offset + count_ref[at, :]
        index = (lane8 - offset) & 127
        near = (lane8 >= offset) & (lane8 < end)
        far = lane8 + LANES < end
        for c in range(2):
            moved = jnp.take_along_axis(ret_ref[pl.ds(d * 16 + c, 8, stride=2), :], index, axis=1, mode="promise_in_bounds")
            for k, keep in enumerate((near, far)):
                for j, piece in enumerate(pieces(jnp.where(keep, moved, 0.0))):
                    shifted[pl.ds(pl.multiple_of(d * 8 + k * LANES, 8), 8), (3 * c + j) * LANES : (3 * c + j + 1) * LANES] = piece
        return carry

    lax.fori_loop(0, LANES // 8, shift, 0, unroll=16)
    row_of = line_ref[0:1, :] >> 7
    sub_rows = iota((chunks, LANES), 0)
    pick = jnp.concatenate([jnp.where(row_of + k == sub_rows, 1.0, 0.0) for k in range(2)], axis=1).astype(BF16)
    spread = jnp.dot(pick, shifted[...].astype(BF16), preferred_element_type=F32)
    for c in range(2):
        part = [spread[:, (3 * c + j) * LANES : (3 * c + j + 1) * LANES] for j in range(3)]
        dense[c * chunks : (c + 1) * chunks, :] = part[0] + (part[1] + part[2])

    line_weight = weight_ref[...] * mask_ref[step_index : step_index + 1, :].astype(F32)
    for d in range(chunks // 8):
        order = order_ref[8 * d : 8 * d + 8, :]
        found = lookup_rows(dense, [0, chunks], chunks, order >> 7, order & 127, 2)
        for c in range(2):
            for s in range(8):
                r = 8 * d + s
                back[c : c + 1, r * LANES : (r + 1) * LANES] = found[c][s : s + 1]
    for e in range(exps):
        at = slice(e * width, (e + 1) * width)
        weighted = (design_ref[:, at].astype(F32) * line_weight[:, at]).astype(BF16)
        residual = (back[:, at] - pred_ref[:, at]).astype(BF16)
        right_ref[e] = lax.dot_general(residual, weighted, NT, preferred_element_type=F32)


def right_sides(k, ret, order, start, count, line, pred, design, weight, mask, exps):
    terms, rows = design.shape
    chunks = rows // LANES
    return call(
        functools.partial(right_body, k),
        jax.ShapeDtypeStruct((exps, 2, terms), F32),
        (
            pltpu.VMEM((2 * LANES, 6 * LANES), F32),
            pltpu.VMEM((2 * chunks, LANES), F32),
            pltpu.VMEM((2, rows), F32),
        ),
        micros=2,
        size=2 * design.size,
    )(ret, order, start, count, line, pred, design, weight, mask)


def exposure_gram(k, design_ref, weight_ref, mask_ref):
    design = design_ref[...]
    weight = weight_ref[...] * mask_ref[k : k + 1, :].astype(F32)
    weighted = (design.astype(F32) * weight).astype(BF16)
    return 0.5 * lax.dot_general(
        jnp.concatenate([weighted, design], axis=1),
        jnp.concatenate([design, weighted], axis=1),
        NT,
        preferred_element_type=F32,
    )


def pack(gram, out_ref):
    terms = gram.shape[0]
    rest = terms - LANES
    out_ref[0, :terms, :] = gram[:, :LANES]
    out_ref[0, terms:, :] = jnp.zeros((rest, LANES), F32)
    out_ref[0, terms:, :rest] = gram[LANES:, LANES:]


def gram_body(k, me_ref, design_ref, weight_ref, mask_ref, gram_ref):
    pack(exposure_gram(k, design_ref, weight_ref, mask_ref), gram_ref)


def gram(me, design, weight, mask, k, exps, mine):
    terms, rows = design.shape
    width = rows // exps
    packed = 2 * terms - LANES
    half = exps // 2

    def exposure(d, me_ref):
        return 2 * lax.rem(lax.div(me_ref[0], 2) + d, half) + lax.rem(me_ref[0] + (0 if mine else 1), 2)

    return pl.pallas_call(
        functools.partial(gram_body, k),
        grid_spec=pltpu.PrefetchScalarGridSpec(
            num_scalar_prefetch=1,
            grid=(half,),
            in_specs=[
                pl.BlockSpec((terms, width), lambda d, me_ref: (0, exposure(d, me_ref))),
                pl.BlockSpec((1, width), lambda d, me_ref: (0, exposure(d, me_ref))),
                pl.BlockSpec((2, width), lambda d, me_ref: (0, exposure(d, me_ref))),
            ],
            out_specs=pl.BlockSpec((1, packed, LANES), lambda d, me_ref: (d, 0, 0)),
        ),
        out_shape=jax.ShapeDtypeStruct((half, packed, LANES), F32),
        compiler_params=pltpu.CompilerParams(vmem_limit_bytes=GRANT),
        cost_estimate=pl.CostEstimate(
            flops=2 * FLOPS_PER_US, bytes_accessed=2 * design.size, transcendentals=0
        ),
    )(me, design, weight, mask)


def eliminate(panel, base, tile):
    sub = iota((8, LANES), 0)
    lane = iota((8, LANES), 1)
    panel = list(panel)
    index = jnp.zeros((8, LANES), jnp.int32) + base
    cols = [jnp.take_along_axis(panel[tile], index + j, axis=1, mode="promise_in_bounds") for j in range(8)]
    for j in range(8):
        inverse = 1.0 / jnp.broadcast_to(cols[j][j : j + 1], (8, LANES))
        mine = sub == j
        panel[tile] = jnp.where(lane == base + j, jnp.where(mine, 1.0, 0.0), panel[tile])

        def sweep(x):
            row = jnp.broadcast_to(x[j : j + 1], (8, LANES)) * inverse
            return jnp.where(mine, row, x - cols[j] * row)

        for m in range(j + 1, 8):
            cols[m] = sweep(cols[m])
        panel = [sweep(x) for x in panel]
    inside = (lane >= base) & (lane < base + 8)
    panel[tile] = jnp.where(inside, -panel[tile], panel[tile])
    return panel


def outside(k, rows):
    lane = iota((rows, 2 * LANES), 1)
    return jnp.where((lane >= k * 8) & (lane < k * 8 + 8), 0.0, 1.0)


def block_rows(k):
    return pl.ds(pl.multiple_of(k * 8, 8), 8)


def update_all(mat, k, before, swept):
    r, q = pieces(jnp.concatenate(before, axis=1)), pieces(jnp.concatenate(swept, axis=1))
    left = jnp.concatenate([r[0], r[0], r[0], r[1], r[1], r[2]], axis=0).astype(BF16)
    right = jnp.concatenate([q[0], q[1], q[2], q[0], q[1], q[0]], axis=0).astype(BF16)
    change = lax.dot_general(left, right, TN, preferred_element_type=F32)
    mat[...] = mat[...] * outside(k, 1) - change[: mat.shape[0]]
    mat[block_rows(k), :] = jnp.concatenate(swept, axis=1)


def update_next(mat, k, swept, base, tile):
    at = block_rows(jnp.minimum(k + 1, mat.shape[0] // 8 - 1))
    rows = [mat[at, t * LANES : (t + 1) * LANES] for t in range(2)]
    keep = outside(k, 8)
    index = jnp.zeros((8, LANES), jnp.int32) + base
    fresh = [rows[t] * keep[:, t * LANES : (t + 1) * LANES] for t in range(2)]
    for j in range(8):
        col = jnp.take_along_axis(rows[tile], index + j, axis=1, mode="promise_in_bounds")
        fresh = [fresh[t] - col * jnp.broadcast_to(swept[t][j : j + 1], (8, LANES)) for t in range(2)]
    return fresh


def sweep_range(mat, low, high):
    start = low // 16
    base = low * 8 - start * LANES
    first = [mat[low * 8 : low * 8 + 8, t * LANES : (t + 1) * LANES] for t in range(2)]
    swept = eliminate(first, base, start)
    carry = (tuple(first), tuple(swept), tuple(update_next(mat, low, swept, base, start)))
    for tile in range(2):
        begin, end = max(low + 1, 16 * tile), min(high, 16 * (tile + 1))

        def step(k, carry):
            before, swept, panel = carry
            base = k * 8 - tile * LANES
            fresh = eliminate(panel, base, tile)
            update_all(mat, k - 1, before, swept)
            return (panel, tuple(fresh), tuple(update_next(mat, k, fresh, base, tile)))

        if begin < end:
            carry = lax.fori_loop(begin, end, step, carry, unroll=3)
    update_all(mat, high - 1, carry[0], carry[1])


def unpack(gram_refs, mat):
    terms = mat.shape[0]
    rest = terms - LANES
    total = functools.reduce(lambda a, b: a + b, [ref[...] for ref in gram_refs])
    square = jnp.concatenate([total[LANES:terms], jnp.zeros((LANES - rest, LANES), F32)], axis=0)
    mat[:, :LANES] = total[:terms]
    mat[:LANES, LANES:] = square.T
    mat[LANES:, LANES:] = total[terms:]
    mat[...] = mat[...] + jnp.where(iota((terms, 2 * LANES), 0) == iota((terms, 2 * LANES), 1), RIDGE, 0.0)


def invert_body(*refs):
    *gram_refs, out_ref, mat = refs
    unpack(gram_refs, mat)
    sweep_range(mat, 0, mat.shape[0] // 8)
    out_ref[...] = -mat[...]


def invert(grams, terms):
    return call(
        invert_body,
        pltpu.HBM((terms, 2 * LANES), F32),
        (pltpu.VMEM((terms, 2 * LANES), F32),),
        micros=8,
        size=4 * len(grams) * grams[0].size,
    )(*grams)


def invert_first_body(high, *refs):
    *gram_refs, mat = refs
    unpack(gram_refs, mat)
    sweep_range(mat, 0, high)


def invert_rest_body(low, part_ref, out_ref):
    out_ref[...] = part_ref[...]
    sweep_range(out_ref, low, out_ref.shape[0] // 8)
    out_ref[...] = -out_ref[...]


def invert_first(grams, terms, high):
    return call(
        functools.partial(invert_first_body, high),
        jax.ShapeDtypeStruct((terms, 2 * LANES), F32),
        micros=4,
        size=4 * len(grams) * grams[0].size,
    )(*grams)


def invert_rest(part, low):
    return call(
        functools.partial(invert_rest_body, low),
        jax.ShapeDtypeStruct(part.shape, F32),
        micros=4,
        size=8 * part.size,
    )(part)


def solve_body(last, *refs):
    if last:
        me_ref, coef_ref, right_ref, inverse_ref, out_ref = refs
    else:
        right_ref, inverse_ref, out_ref = refs
    terms = inverse_ref.shape[0]
    right = right_ref[0]
    for s in range(1, right_ref.shape[0]):
        right = right + right_ref[s]
    update = jnp.dot(right, inverse_ref[...], precision=lax.Precision.HIGHEST, preferred_element_type=F32)[:, :terms]
    if last:
        update = coef_ref[me_ref[0]] + update
    for s in range(right_ref.shape[0]):
        out_ref[s] = update


def solve(right, inverse):
    shape = jax.ShapeDtypeStruct(right.shape, F32)
    return call(functools.partial(solve_body, False), shape, micros=1, size=inverse.size * 4)(right, inverse)


def solve_last(me, coef, right, inverse):
    shape = jax.ShapeDtypeStruct(right.shape, F32)
    specs = [pl.BlockSpec(memory_space=pltpu.SMEM)] + [pl.BlockSpec()] * 3
    return call(functools.partial(solve_body, True), shape, micros=1, size=inverse.size * 4, in_specs=specs)(
        me, coef, right, inverse
    )


def on_device(design, det_weight, outlier_mask, star_owner, star_slot, coef_init, star_ref, star_prior):
    everyone = ("pix", "exp")
    peers = lax.axis_size(everyone)
    terms, rows = design.shape
    exps = coef_init.shape[0]
    cap = 2 * rows // peers
    owner = star_owner.reshape(rows // LANES, LANES)
    slot = star_slot.reshape(rows // LANES, LANES)
    weight_rows = det_weight.reshape(rows // LANES, LANES)
    weight_line = det_weight.reshape(1, rows)
    prior = star_prior.reshape(star_prior.shape[0] // LANES, LANES)

    def exchange(x):
        y = lax.all_to_all(x.reshape(peers, -1, LANES), everyone, split_axis=0, concat_axis=0, tiled=True)
        return y.reshape(x.shape)

    def over_pix(x):
        return lax.all_to_all(x, "pix", split_axis=0, concat_axis=0, tiled=True)

    pixes = lax.axis_size("pix")
    me = lax.axis_index("pix").reshape(1)

    def norm_exchange(send, keep):
        got = lax.ppermute(send, "pix", [(i, i ^ 1) for i in range(pixes)])
        parts = []
        for d in range(pixes // 2):
            part = keep[d] + got[d]
            if d > 0:
                part = lax.ppermute(part, "pix", [(i, (i + 2 * d) % pixes) for i in range(pixes)])
            parts.append(part)
        return parts

    order, row, lane, start, count, line = route(owner)
    pred, pay = place_first(coef_init, design, row, lane, start, count, slot, weight_rows, outlier_mask, cap)
    pay = exchange(pay)
    send = gram(me, design, weight_line, outlier_mask, 0, exps, False)
    keep = gram(me, design, weight_line, outlier_mask, 0, exps, True)
    gram_0 = norm_exchange(send, keep)
    ret, kept = owner_first(pay, star_ref, prior, cap)
    ret = exchange(ret)
    inverse_0 = invert_first(gram_0, terms, SPLIT)
    inverse_0 = invert_rest(inverse_0, SPLIT)
    right = right_sides(0, ret, order, start, count, line, pred, design, weight_line, outlier_mask, exps)
    right = over_pix(right)
    send = gram(me, design, weight_line, outlier_mask, 1, exps, False)
    keep = gram(me, design, weight_line, outlier_mask, 1, exps, True)
    gram_1 = norm_exchange(send, keep)
    upd = solve(right, inverse_0)
    upd = over_pix(upd)
    pred, pay, coef = place_next(coef_init, upd, design, row, lane, start, count, cap)
    pay = exchange(pay)
    ret, means = owner_next(pay, kept, star_ref, prior, cap)
    ret = exchange(ret)
    inverse_1 = invert(gram_1, terms)
    right = right_sides(1, ret, order, start, count, line, pred, design, weight_line, outlier_mask, exps)
    right = over_pix(right)
    coef = solve_last(me, coef, right, inverse_1)
    coef = over_pix(coef)
    return (coef, means)


def solution(mesh):
    placed = (
        P(None, ("pix", "exp")),
        P(("pix", "exp")),
        P(None, ("pix", "exp")),
        P(("pix", "exp"), None),
        P(("pix", "exp")),
        P("exp", None, None),
        P(None, ("pix", "exp")),
        P(("pix", "exp")),
    )
    return jax.shard_map(
        on_device,
        mesh=mesh,
        in_specs=placed,
        out_specs=(P("exp", None, None), P(None, ("pix", "exp"))),
        check_vma=False,
    )
```

```python
import functools

import jax
import jax.numpy as jnp
from jax import lax
from jax.experimental import pallas as pl
from jax.experimental.pallas import tpu as pltpu
from jax.sharding import PartitionSpec as P


RIDGE = 0.5
LANES = 128
F32 = jnp.float32
BF16 = jnp.bfloat16
GRANT = 16 << 20
FLOPS_PER_US = 10**9
SPLIT = 8
NT = (((1,), (1,)), ((), ()))
TN = (((0,), (0,)), ((), ()))


def iota(shape, axis):
    return lax.broadcasted_iota(jnp.int32, shape, axis)


def lane_gather(row, index):
    table = jnp.broadcast_to(row, index.shape)
    return jnp.take_along_axis(table, index, axis=1, mode="promise_in_bounds")


def call(body, out_shape, scratch=(), micros=1, size=0, in_specs=None):
    specs = {} if in_specs is None else {"in_specs": in_specs}
    return pl.pallas_call(
        body,
        **specs,
        out_shape=out_shape,
        scratch_shapes=list(scratch),
        compiler_params=pltpu.CompilerParams(vmem_limit_bytes=GRANT),
        cost_estimate=pl.CostEstimate(flops=micros * FLOPS_PER_US, bytes_accessed=size, transcendentals=0),
    )


def route_body(owner_ref, order_ref, row_ref, lane_ref, start_ref, count_ref, line_ref, hot_ref, left_ref, right_ref):
    chunks = owner_ref.shape[0]
    sub = iota((LANES, LANES), 0)
    lane = iota((LANES, LANES), 1)
    wide_sub, wide_lane = iota((LANES, 2 * LANES), 0), iota((LANES, 2 * LANES), 1)
    prefix = jnp.where((wide_sub < wide_lane) | (wide_lane >= LANES), 1.0, 0.0).astype(BF16)

    def rank(r, base):
        at = pl.ds(pl.multiple_of(r * LANES, LANES), LANES)
        hot = jnp.where(owner_ref[pl.ds(r, 1), :] == sub, 1.0, 0.0)
        narrow = hot.astype(BF16)
        hot_ref[:, at] = narrow
        counts = jnp.dot(narrow, prefix, preferred_element_type=F32)
        order_ref[pl.ds(r, 1), :] = jnp.sum(hot * (counts[:, :LANES] + base), axis=0, keepdims=True).astype(jnp.int32)
        return base + counts[:, LANES:]

    counts = lax.fori_loop(0, chunks, rank, jnp.zeros((LANES, LANES), F32), unroll=48)
    high = jnp.floor(counts * (1.0 / LANES))
    split = jnp.concatenate([high, counts - high * LANES], axis=1).astype(BF16)
    below = jnp.where(lane < sub, 1.0, 0.0).astype(BF16)
    starts = jnp.dot(below, split, preferred_element_type=F32)
    start_ref[...] = (starts[:, :LANES] * LANES + starts[:, LANES:]).astype(jnp.int32)
    count_ref[...] = counts.astype(jnp.int32)
    line = jnp.sum(jnp.where(sub < lane, counts, 0.0), axis=0, keepdims=True)
    line8 = jnp.broadcast_to(line, (8, LANES))
    line_ref[...] = line8.astype(jnp.int32)
    high8 = jnp.floor(line8 * (1.0 / LANES))
    first = jnp.where(iota((8, LANES), 0) == 0, high8, line8 - high8 * LANES).astype(BF16)
    begin = jnp.dot(first, hot_ref[...], preferred_element_type=F32)
    sub_rows, lane_line = iota((chunks, LANES), 0), iota((1, LANES), 1).astype(F32)
    for r in range(chunks):
        at = slice(r * LANES, (r + 1) * LANES)
        place = order_ref[r : r + 1, :] + (begin[0:1, at] * LANES + begin[1:2, at]).astype(jnp.int32)
        order_ref[r : r + 1, :] = place
        hit = jnp.where((place >> 7) == sub_rows, 1.0, 0.0)
        left_ref[:chunks, at] = (hit * float(r)).astype(BF16)
        left_ref[chunks:, at] = (hit * lane_line).astype(BF16)
        right_ref[:, at] = jnp.where((place & 127) == sub, 1.0, 0.0).astype(BF16)
    held = lax.dot_general(left_ref[...], right_ref[...], NT, preferred_element_type=F32)
    row_ref[...] = held[:chunks].astype(jnp.int32)
    lane_ref[...] = held[chunks:].astype(jnp.int32)


def route(owner):
    chunks = owner.shape[0]
    rows = chunks * LANES
    line = jax.ShapeDtypeStruct(owner.shape, jnp.int32)
    plane = jax.ShapeDtypeStruct((LANES, LANES), jnp.int32)
    return call(
        route_body,
        (line, line, line, plane, plane, jax.ShapeDtypeStruct((8, LANES), jnp.int32)),
        (pltpu.VMEM((LANES, rows), BF16), pltpu.VMEM((2 * chunks, rows), BF16), pltpu.VMEM((LANES, rows), BF16)),
        micros=4,
        size=rows * 8,
    )(owner)


def pieces(x):
    a = x.astype(BF16).astype(F32)
    b = (x - a).astype(BF16).astype(F32)
    c = ((x - a) - b).astype(BF16).astype(F32)
    return (a, b, c)


def lookup_rows(table, base, chunks, row, lane, values):
    found = [jnp.zeros((8, LANES), F32)] * values
    for r in range(chunks):
        hit = row == r
        for v in range(values):
            at = base[v] + r
            found[v] = jnp.where(hit, lane_gather(table[at : at + 1, :], lane), found[v])
    return found


def place_body(cap, first, *refs):
    if first:
        (coef_ref, design_ref, row_ref, lane_ref, start_ref, count_ref, slot_ref, weight_ref, mask_ref) = refs[:9]
        pred_ref, pay_ref, vals, dense, spread = refs[9:]
        coef = coef_ref[...]
    else:
        coef_ref, upd_ref, design_ref, row_ref, lane_ref, start_ref, count_ref = refs[:7]
        pred_ref, pay_ref, new_ref, vals, dense, spread = refs[7:]
        coef = coef_ref[...] + upd_ref[...]
        new_ref[...] = coef
    exps = coef.shape[0]
    rows = design_ref.shape[1]
    chunks = rows // LANES
    width = rows // exps
    per = width // LANES
    maps = coef.astype(BF16)
    for e in range(exps):
        pred = jnp.dot(maps[e], design_ref[:, e * width : (e + 1) * width], preferred_element_type=F32)
        pred_ref[:, e * width : (e + 1) * width] = pred
        for c in range(2):
            for q in range(per):
                r = c * chunks + e * per + q
                vals[r : r + 1, :] = pred[c : c + 1, q * LANES : (q + 1) * LANES]
    if first:
        for r in range(chunks):
            at = slice(r * LANES, (r + 1) * LANES)
            code = slot_ref[r : r + 1, :] + (mask_ref[0:1, at] << 10) + (mask_ref[1:2, at] << 11)
            vals[2 * chunks + r : 2 * chunks + r + 1, :] = code.astype(F32)
        vals[3 * chunks : 4 * chunks, :] = weight_ref[...]
    values = 4 if first else 2
    width_out = 4 if first else 2
    lane8 = iota((8, LANES), 1)

    def gather(d, carry):
        at = pl.ds(pl.multiple_of(d * 8, 8), 8)
        found = lookup_rows(vals, [v * chunks for v in range(values)], chunks, row_ref[at, :], lane_ref[at, :], values)
        for v in range(values):
            for k, piece in enumerate(pieces(found[v])):
                dense[at, (3 * v + k) * LANES : (3 * v + k + 1) * LANES] = piece
        return carry

    lax.fori_loop(0, chunks // 8, gather, 0, unroll=6)
    row_of = start_ref[...] >> 7
    column = iota((LANES, chunks), 1)
    pick = jnp.concatenate(
        [jnp.where(row_of[:, :chunks] + k == column, 1.0, 0.0) for k in range(2)], axis=0
    ).astype(BF16)
    spread[...] = jnp.dot(pick, dense[...].astype(BF16), preferred_element_type=F32)

    def tile(d, carry):
        at = pl.ds(pl.multiple_of(d * 8, 8), 8)
        spot = (start_ref[at, :] & 127) + lane8
        index, near = spot & 127, spot < LANES
        held = lane8 < count_ref[at, :]
        found = []
        for v in range(values):
            rows_of = []
            for k in range(2):
                part = [
                    spread[pl.ds(pl.multiple_of(d * 8 + k * LANES, 8), 8), (3 * v + j) * LANES : (3 * v + j + 1) * LANES]
                    for j in range(3)
                ]
                whole = part[0] + (part[1] + part[2])
                rows_of.append(jnp.take_along_axis(whole, index, axis=1, mode="promise_in_bounds"))
            found.append(jnp.where(held, jnp.where(near, rows_of[0], rows_of[1]), 0.0))
        if first:
            spare = LANES - cap
            code, weight = found[2].astype(jnp.int32), found[3]
            found[2] = (code & 1023).astype(F32)
            found[3] = weight * ((code >> 10) & 1).astype(F32)
            later = weight * (code >> 11).astype(F32)
            for v in range(3):
                moved = pltpu.roll(later, (cap - v * spare) % LANES, 1)
                found[v] = jnp.where(lane8 < cap, found[v], moved)
        for v in range(width_out):
            pay_ref[pl.ds(d * 8 * width_out + v, 8, stride=width_out), :] = found[v]
        return carry

    lax.fori_loop(0, LANES // 8, tile, 0, unroll=8 if first else 16)


def place_scratch(values, chunks):
    return (
        pltpu.VMEM((values * chunks, LANES), F32),
        pltpu.VMEM((chunks, 3 * values * LANES), F32),
        pltpu.VMEM((2 * LANES, 3 * values * LANES), F32),
    )


def place_first(coef, design, row, lane, start, count, slot, weight, mask, cap):
    rows = design.shape[1]
    return call(
        functools.partial(place_body, cap, True),
        (pltpu.HBM((2, rows), F32), jax.ShapeDtypeStruct((4 * LANES, LANES), F32)),
        place_scratch(4, rows // LANES),
        micros=5,
        size=2 * design.size,
    )(coef, design, row, lane, start, count, slot, weight, mask)


def place_next(coef, upd, design, row, lane, start, count, cap):
    rows = design.shape[1]
    return call(
        functools.partial(place_body, cap, False),
        (
            pltpu.HBM((2, rows), F32),
            jax.ShapeDtypeStruct((2 * LANES, LANES), F32),
            jax.ShapeDtypeStruct(coef.shape, F32),
        ),
        place_scratch(2, rows // LANES),
        micros=3,
        size=2 * design.size,
    )(coef, upd, design, row, lane, start, count)


def owner_body(cap, first, *refs):
    if first:
        pay_ref, ref_ref, prior_ref, ret_ref, kept_ref, parts, id_ref = refs
        width = 4
    else:
        pay_ref, kept_ref, ref_ref, prior_ref, ret_ref, mean_ref, parts, id_ref = refs
        width = 2
    lane8 = iota((8, LANES), 1)
    sub8 = iota((8, LANES), 0)
    sub = iota((LANES, LANES), 0)
    spare = LANES - cap

    def split(g, carry):
        def plane(v):
            return pay_ref[pl.ds(g * 8 * width + v, 8, stride=width), :]

        at = pl.ds(pl.multiple_of(g * 8, 8), 8)
        if first:
            p0, p1, ids, weight = plane(0), plane(1), plane(2), plane(3)
            later = jnp.zeros((8, LANES), F32)
            for v, source in enumerate((p0, p1, ids)):
                moved = pltpu.roll(source, (v * spare - cap) % LANES, 1)
                later = jnp.where((lane8 >= v * spare) & (lane8 < (v + 1) * spare), moved, later)
            kept_ref[0, at, :] = ids
            kept_ref[1, at, :] = later
            weight = jnp.where(lane8 < cap, weight, 0.0)
            id_ref[at, :] = ids.astype(jnp.int32)
        else:
            p0, p1, weight = plane(0), plane(1), kept_ref[1, at, :]
            id_ref[at, :] = kept_ref[0, at, :].astype(jnp.int32)
        for v, x in enumerate((weight * p0, weight * p1, weight)):
            for k, piece in enumerate(pieces(x)):
                parts[3 * v + k, at, :] = piece
        return carry

    lax.fori_loop(0, LANES // 8, split, 0, unroll=16)
    group = 8

    def accumulate(g, total):
        left, right = [], []
        for s in range(group):
            src = g * group + s
            ids = id_ref[pl.ds(src, 1), :]
            hit = (ids >> 7) == sub8
            left.append(
                jnp.concatenate(
                    [jnp.where(hit, parts[k, pl.ds(src, 1), :], 0.0) for k in range(9)], axis=0
                ).astype(BF16)
            )
            right.append(jnp.where((ids & 127) == sub, 1.0, 0.0).astype(BF16))
        return total + lax.dot_general(
            jnp.concatenate(right, axis=1), jnp.concatenate(left, axis=1), NT, preferred_element_type=F32
        )

    total = lax.fori_loop(0, LANES // group, accumulate, jnp.zeros((LANES, 72), F32), unroll=16).T
    sums = [total[24 * v : 24 * v + 8] + total[24 * v + 8 : 24 * v + 16] + total[24 * v + 16 : 24 * v + 24] for v in range(3)]
    rows = prior_ref.shape[0]
    means = [[], []]
    for h in range(rows):
        prior = prior_ref[h : h + 1, :]
        for c in range(2):
            ref = ref_ref[c : c + 1, h * LANES : (h + 1) * LANES]
            mean = (prior * ref + sums[c][h : h + 1]) / (prior + sums[2][h : h + 1])
            means[c].append(mean)
            if not first:
                mean_ref[c : c + 1, h * LANES : (h + 1) * LANES] = mean

    def look(g, carry):
        at = pl.ds(pl.multiple_of(g * 8, 8), 8)
        ids = id_ref[at, :]
        low, high = ids & 127, ids >> 7
        for c in range(2):
            found = jnp.zeros((8, LANES), F32)
            for h in range(rows):
                found = jnp.where(high == h, lane_gather(means[c][h], low), found)
            ret_ref[pl.ds(g * 16 + c, 8, stride=2), :] = found
        return carry

    lax.fori_loop(0, LANES // 8, look, 0, unroll=16)


def owner_first(pay, star_ref, star_prior, cap):
    return call(
        functools.partial(owner_body, cap, True),
        (
            jax.ShapeDtypeStruct((2 * LANES, LANES), F32),
            pltpu.HBM((2, LANES, LANES), F32),
        ),
        (pltpu.VMEM((9, LANES, LANES), F32), pltpu.VMEM((LANES, LANES), jnp.int32)),
        micros=4,
        size=pay.size * 4,
    )(pay, star_ref, star_prior)


def owner_next(pay, kept, star_ref, star_prior, cap):
    return call(
        functools.partial(owner_body, cap, False),
        (jax.ShapeDtypeStruct((2 * LANES, LANES), F32), jax.ShapeDtypeStruct(star_ref.shape, F32)),
        (
            pltpu.VMEM((9, LANES, LANES), F32),
            pltpu.VMEM((LANES, LANES), jnp.int32),
        ),
        micros=3,
        size=pay.size * 4,
    )(pay, kept, star_ref, star_prior)


def right_body(step_index, *refs):
    ret_ref, order_ref, start_ref, count_ref, line_ref, pred_ref, design_ref, weight_ref, mask_ref = refs[:9]
    right_ref, shifted, dense, back = refs[9:]
    chunks = order_ref.shape[0]
    exps = right_ref.shape[0]
    rows = pred_ref.shape[1]
    width = rows // exps
    lane8 = iota((8, LANES), 1)

    def shift(d, carry):
        at = pl.ds(pl.multiple_of(d * 8, 8), 8)
        offset = start_ref[at, :] & 127
        end = offset + count_ref[at, :]
        index = (lane8 - offset) & 127
        near = (lane8 >= offset) & (lane8 < end)
        far = lane8 + LANES < end
        for c in range(2):
            moved = jnp.take_along_axis(ret_ref[pl.ds(d * 16 + c, 8, stride=2), :], index, axis=1, mode="promise_in_bounds")
            for k, keep in enumerate((near, far)):
                for j, piece in enumerate(pieces(jnp.where(keep, moved, 0.0))):
                    shifted[pl.ds(pl.multiple_of(d * 8 + k * LANES, 8), 8), (3 * c + j) * LANES : (3 * c + j + 1) * LANES] = piece
        return carry

    lax.fori_loop(0, LANES // 8, shift, 0, unroll=16)
    row_of = line_ref[0:1, :] >> 7
    sub_rows = iota((chunks, LANES), 0)
    pick = jnp.concatenate([jnp.where(row_of + k == sub_rows, 1.0, 0.0) for k in range(2)], axis=1).astype(BF16)
    spread = jnp.dot(pick, shifted[...].astype(BF16), preferred_element_type=F32)
    for c in range(2):
        part = [spread[:, (3 * c + j) * LANES : (3 * c + j + 1) * LANES] for j in range(3)]
        dense[c * chunks : (c + 1) * chunks, :] = part[0] + (part[1] + part[2])

    line_weight = weight_ref[...] * mask_ref[step_index : step_index + 1, :].astype(F32)
    for d in range(chunks // 8):
        order = order_ref[8 * d : 8 * d + 8, :]
        found = lookup_rows(dense, [0, chunks], chunks, order >> 7, order & 127, 2)
        for c in range(2):
            for s in range(8):
                r = 8 * d + s
                back[c : c + 1, r * LANES : (r + 1) * LANES] = found[c][s : s + 1]
    for e in range(exps):
        at = slice(e * width, (e + 1) * width)
        weighted = (design_ref[:, at].astype(F32) * line_weight[:, at]).astype(BF16)
        residual = (back[:, at] - pred_ref[:, at]).astype(BF16)
        right_ref[e] = lax.dot_general(residual, weighted, NT, preferred_element_type=F32)


def right_sides(k, ret, order, start, count, line, pred, design, weight, mask, exps):
    terms, rows = design.shape
    chunks = rows // LANES
    return call(
        functools.partial(right_body, k),
        jax.ShapeDtypeStruct((exps, 2, terms), F32),
        (
            pltpu.VMEM((2 * LANES, 6 * LANES), F32),
            pltpu.VMEM((2 * chunks, LANES), F32),
            pltpu.VMEM((2, rows), F32),
        ),
        micros=2,
        size=2 * design.size,
    )(ret, order, start, count, line, pred, design, weight, mask)


def exposure_gram(k, design_ref, weight_ref, mask_ref):
    design = design_ref[...]
    weight = weight_ref[...] * mask_ref[k : k + 1, :].astype(F32)
    weighted = (design.astype(F32) * weight).astype(BF16)
    return 0.5 * lax.dot_general(
        jnp.concatenate([weighted, design], axis=1),
        jnp.concatenate([design, weighted], axis=1),
        NT,
        preferred_element_type=F32,
    )


def pack(gram, out_ref):
    terms = gram.shape[0]
    rest = terms - LANES
    out_ref[0, :terms, :] = gram[:, :LANES]
    out_ref[0, terms:, :] = jnp.zeros((rest, LANES), F32)
    out_ref[0, terms:, :rest] = gram[LANES:, LANES:]


def gram_body(k, me_ref, design_ref, weight_ref, mask_ref, gram_ref):
    pack(exposure_gram(k, design_ref, weight_ref, mask_ref), gram_ref)


def gram(me, design, weight, mask, k, exps, mine):
    terms, rows = design.shape
    width = rows // exps
    packed = 2 * terms - LANES
    half = exps // 2

    def exposure(d, me_ref):
        return 2 * lax.rem(lax.div(me_ref[0], 2) + d, half) + lax.rem(me_ref[0] + (0 if mine else 1), 2)

    return pl.pallas_call(
        functools.partial(gram_body, k),
        grid_spec=pltpu.PrefetchScalarGridSpec(
            num_scalar_prefetch=1,
            grid=(half,),
            in_specs=[
                pl.BlockSpec((terms, width), lambda d, me_ref: (0, exposure(d, me_ref))),
                pl.BlockSpec((1, width), lambda d, me_ref: (0, exposure(d, me_ref))),
                pl.BlockSpec((2, width), lambda d, me_ref: (0, exposure(d, me_ref))),
            ],
            out_specs=pl.BlockSpec((1, packed, LANES), lambda d, me_ref: (d, 0, 0)),
        ),
        out_shape=jax.ShapeDtypeStruct((half, packed, LANES), F32),
        compiler_params=pltpu.CompilerParams(vmem_limit_bytes=GRANT),
        cost_estimate=pl.CostEstimate(
            flops=2 * FLOPS_PER_US, bytes_accessed=2 * design.size, transcendentals=0
        ),
    )(me, design, weight, mask)


def eliminate(panel, base, tile):
    sub = iota((8, LANES), 0)
    lane = iota((8, LANES), 1)
    panel = list(panel)
    index = jnp.zeros((8, LANES), jnp.int32) + base
    cols = [jnp.take_along_axis(panel[tile], index + j, axis=1, mode="promise_in_bounds") for j in range(8)]
    for j in range(8):
        inverse = 1.0 / jnp.broadcast_to(cols[j][j : j + 1], (8, LANES))
        mine = sub == j
        panel[tile] = jnp.where(lane == base + j, jnp.where(mine, 1.0, 0.0), panel[tile])

        def sweep(x):
            row = jnp.broadcast_to(x[j : j + 1], (8, LANES)) * inverse
            return jnp.where(mine, row, x - cols[j] * row)

        for m in range(j + 1, 8):
            cols[m] = sweep(cols[m])
        panel = [sweep(x) for x in panel]
    inside = (lane >= base) & (lane < base + 8)
    panel[tile] = jnp.where(inside, -panel[tile], panel[tile])
    return panel


def outside(k, rows):
    lane = iota((rows, 2 * LANES), 1)
    return jnp.where((lane >= k * 8) & (lane < k * 8 + 8), 0.0, 1.0)


def block_rows(k):
    return pl.ds(pl.multiple_of(k * 8, 8), 8)


def update_all(mat, k, before, swept):
    r, q = pieces(jnp.concatenate(before, axis=1)), pieces(jnp.concatenate(swept, axis=1))
    left = jnp.concatenate([r[0], r[0], r[0], r[1], r[1], r[2]], axis=0).astype(BF16)
    right = jnp.concatenate([q[0], q[1], q[2], q[0], q[1], q[0]], axis=0).astype(BF16)
    change = lax.dot_general(left, right, TN, preferred_element_type=F32)
    mat[...] = mat[...] * outside(k, 1) - change[: mat.shape[0]]
    mat[block_rows(k), :] = jnp.concatenate(swept, axis=1)


def update_next(mat, k, swept, base, tile):
    at = block_rows(jnp.minimum(k + 1, mat.shape[0] // 8 - 1))
    rows = [mat[at, t * LANES : (t + 1) * LANES] for t in range(2)]
    keep = outside(k, 8)
    index = jnp.zeros((8, LANES), jnp.int32) + base
    fresh = [rows[t] * keep[:, t * LANES : (t + 1) * LANES] for t in range(2)]
    for j in range(8):
        col = jnp.take_along_axis(rows[tile], index + j, axis=1, mode="promise_in_bounds")
        fresh = [fresh[t] - col * jnp.broadcast_to(swept[t][j : j + 1], (8, LANES)) for t in range(2)]
    return fresh


def sweep_range(mat, low, high):
    start = low // 16
    base = low * 8 - start * LANES
    first = [mat[low * 8 : low * 8 + 8, t * LANES : (t + 1) * LANES] for t in range(2)]
    swept = eliminate(first, base, start)
    carry = (tuple(first), tuple(swept), tuple(update_next(mat, low, swept, base, start)))
    for tile in range(2):
        begin, end = max(low + 1, 16 * tile), min(high, 16 * (tile + 1))

        def step(k, carry):
            before, swept, panel = carry
            base = k * 8 - tile * LANES
            fresh = eliminate(panel, base, tile)
            update_all(mat, k - 1, before, swept)
            return (panel, tuple(fresh), tuple(update_next(mat, k, fresh, base, tile)))

        if begin < end:
            carry = lax.fori_loop(begin, end, step, carry, unroll=5)
    update_all(mat, high - 1, carry[0], carry[1])


def unpack(gram_refs, mat):
    terms = mat.shape[0]
    rest = terms - LANES
    total = functools.reduce(lambda a, b: a + b, [ref[...] for ref in gram_refs])
    square = jnp.concatenate([total[LANES:terms], jnp.zeros((LANES - rest, LANES), F32)], axis=0)
    mat[:, :LANES] = total[:terms]
    mat[:LANES, LANES:] = square.T
    mat[LANES:, LANES:] = total[terms:]
    mat[...] = mat[...] + jnp.where(iota((terms, 2 * LANES), 0) == iota((terms, 2 * LANES), 1), RIDGE, 0.0)


def invert_body(*refs):
    *gram_refs, out_ref, mat = refs
    unpack(gram_refs, mat)
    sweep_range(mat, 0, mat.shape[0] // 8)
    out_ref[...] = -mat[...]


def invert(grams, terms):
    return call(
        invert_body,
        pltpu.HBM((terms, 2 * LANES), F32),
        (pltpu.VMEM((terms, 2 * LANES), F32),),
        micros=8,
        size=4 * len(grams) * grams[0].size,
    )(*grams)


def invert_first_body(high, *refs):
    *gram_refs, mat = refs
    unpack(gram_refs, mat)
    sweep_range(mat, 0, high)


def invert_rest_body(low, part_ref, out_ref):
    out_ref[...] = part_ref[...]
    sweep_range(out_ref, low, out_ref.shape[0] // 8)
    out_ref[...] = -out_ref[...]


def invert_first(grams, terms, high):
    return call(
        functools.partial(invert_first_body, high),
        jax.ShapeDtypeStruct((terms, 2 * LANES), F32),
        micros=4,
        size=4 * len(grams) * grams[0].size,
    )(*grams)


def invert_rest(part, low):
    return call(
        functools.partial(invert_rest_body, low),
        jax.ShapeDtypeStruct(part.shape, F32),
        micros=4,
        size=8 * part.size,
    )(part)


def solve_body(last, *refs):
    if last:
        me_ref, coef_ref, right_ref, inverse_ref, out_ref = refs
    else:
        right_ref, inverse_ref, out_ref = refs
    terms = inverse_ref.shape[0]
    right = right_ref[0]
    for s in range(1, right_ref.shape[0]):
        right = right + right_ref[s]
    update = jnp.dot(right, inverse_ref[...], precision=lax.Precision.HIGHEST, preferred_element_type=F32)[:, :terms]
    if last:
        update = coef_ref[me_ref[0]] + update
    for s in range(right_ref.shape[0]):
        out_ref[s] = update


def solve(right, inverse):
    shape = jax.ShapeDtypeStruct(right.shape, F32)
    return call(functools.partial(solve_body, False), shape, micros=1, size=inverse.size * 4)(right, inverse)


def solve_last(me, coef, right, inverse):
    shape = jax.ShapeDtypeStruct(right.shape, F32)
    specs = [pl.BlockSpec(memory_space=pltpu.SMEM)] + [pl.BlockSpec()] * 3
    return call(functools.partial(solve_body, True), shape, micros=1, size=inverse.size * 4, in_specs=specs)(
        me, coef, right, inverse
    )


def on_device(design, det_weight, outlier_mask, star_owner, star_slot, coef_init, star_ref, star_prior):
    everyone = ("pix", "exp")
    peers = lax.axis_size(everyone)
    terms, rows = design.shape
    exps = coef_init.shape[0]
    cap = 2 * rows // peers
    owner = star_owner.reshape(rows // LANES, LANES)
    slot = star_slot.reshape(rows // LANES, LANES)
    weight_rows = det_weight.reshape(rows // LANES, LANES)
    weight_line = det_weight.reshape(1, rows)
    prior = star_prior.reshape(star_prior.shape[0] // LANES, LANES)

    def exchange(x):
        y = lax.all_to_all(x.reshape(peers, -1, LANES), everyone, split_axis=0, concat_axis=0, tiled=True)
        return y.reshape(x.shape)

    def over_pix(x):
        return lax.all_to_all(x, "pix", split_axis=0, concat_axis=0, tiled=True)

    pixes = lax.axis_size("pix")
    me = lax.axis_index("pix").reshape(1)

    def norm_exchange(send, keep):
        got = lax.ppermute(send, "pix", [(i, i ^ 1) for i in range(pixes)])
        parts = []
        for d in range(pixes // 2):
            part = keep[d] + got[d]
            if d > 0:
                part = lax.ppermute(part, "pix", [(i, (i + 2 * d) % pixes) for i in range(pixes)])
            parts.append(part)
        return parts

    order, row, lane, start, count, line = route(owner)
    pred, pay = place_first(coef_init, design, row, lane, start, count, slot, weight_rows, outlier_mask, cap)
    pay = exchange(pay)
    send = gram(me, design, weight_line, outlier_mask, 0, exps, False)
    keep = gram(me, design, weight_line, outlier_mask, 0, exps, True)
    gram_0 = norm_exchange(send, keep)
    ret, kept = owner_first(pay, star_ref, prior, cap)
    ret = exchange(ret)
    inverse_0 = invert_first(gram_0, terms, SPLIT)
    inverse_0 = invert_rest(inverse_0, SPLIT)
    right = right_sides(0, ret, order, start, count, line, pred, design, weight_line, outlier_mask, exps)
    right = over_pix(right)
    send = gram(me, design, weight_line, outlier_mask, 1, exps, False)
    keep = gram(me, design, weight_line, outlier_mask, 1, exps, True)
    gram_1 = norm_exchange(send, keep)
    upd = solve(right, inverse_0)
    upd = over_pix(upd)
    pred, pay, coef = place_next(coef_init, upd, design, row, lane, start, count, cap)
    pay = exchange(pay)
    ret, means = owner_next(pay, kept, star_ref, prior, cap)
    ret = exchange(ret)
    inverse_1 = invert(gram_1, terms)
    right = right_sides(1, ret, order, start, count, line, pred, design, weight_line, outlier_mask, exps)
    right = over_pix(right)
    coef = solve_last(me, coef, right, inverse_1)
    coef = over_pix(coef)
    return (coef, means)


def solution(mesh):
    placed = (
        P(None, ("pix", "exp")),
        P(("pix", "exp")),
        P(None, ("pix", "exp")),
        P(("pix", "exp"), None),
        P(("pix", "exp")),
        P("exp", None, None),
        P(None, ("pix", "exp")),
        P(("pix", "exp")),
    )
    return jax.shard_map(
        on_device,
        mesh=mesh,
        in_specs=placed,
        out_specs=(P("exp", None, None), P(None, ("pix", "exp"))),
        check_vma=False,
    )
```
